256 devices in a mesh: fsdp: 64 (over z_lo, x, y, core), tensor: 4 (over z_hi).
Axes of the slice: x: 4, y: 4, z: 8 (z_hi: 4, z_lo: 2; z = z_hi * 2 + z_lo), core: 2. Of those that a mesh axis runs over, the one named last changes fastest.
Arguments:
- normed: bfloat16 [65536, 8192], P('fsdp', 'tensor')
- tile_values: bfloat16 [4, 128, 128, 128], P('tensor', 'fsdp'), may hold values from -0.09375 to 0.09375
- tile_rows: int32 [4, 128], P('tensor', 'fsdp'), may hold values from -1 to 15, as said below
- tile_columns: int32 [4, 128], P('tensor', 'fsdp'), may hold values from -1 to 7, as said below
- cotangent: bfloat16 [65536, 1024], P('fsdp', 'tensor')
Outputs:
- values: bfloat16 [65536, 1024], P('fsdp', 'tensor')
- grad_input: bfloat16 [65536, 8192], P('fsdp', 'tensor')
- tile_update: bfloat16 [4, 128, 128, 128], P('tensor', 'fsdp')
The draws below stay inside these ranges and needn't reach their ends.
Inputs may be any that keep to these rules, and one draw needn't show every extreme that they name: tile_rows[q, s] is -1 exactly where tile_columns[q, s] is -1 (an empty slot). In every part q exactly 64 slots are filled, no (row block, column block) pair appears twice, and each column block holds exactly 8 of the 16 row blocks. The slots s with equal s // 2 belong to one owner; in every part some owner has all 2 of its slots filled. `tile_columns`: column block of the tile in each slot; -1 marks an empty slot, as in tile_rows.
All inputs are finite; a program needn't handle non-finite values.
Results may differ from the reference program's by a relative error of at most 0.001.
Values may be sent and summed in bfloat16 or wider, within the bound.
A program may use at most 128 MiB of HBM per device.

```python
import jax
import jax.numpy as jnp
from jax import lax

D = 8192
KVW = 1024
TILE = 128
QUARTERS = 4
RB = 16
CB = 8
KEPT = 64
CAP = 2
SLOTS = 128
TOKENS = 65536


def feature_draw(key, row_total, feature_total):
    noise_key, scale_key = jax.random.split(key, 2)
    scales = jnp.exp(jax.random.uniform(scale_key, (feature_total,), jnp.float32, -1.15, 1.15))
    noise = jax.random.normal(noise_key, (row_total, feature_total), jnp.float32)
    return (noise * scales[None, :]).astype(jnp.bfloat16)


def draw_normed(key, part):
    return feature_draw(jax.random.fold_in(key, 3), TOKENS, D)


def draw_cotangent(key, part):
    return feature_draw(jax.random.fold_in(key, 5), TOKENS, KVW)


def quarter_layout(quarter_key):
    pick_key, shuffle_key, owner_key, spread_key = jax.random.split(quarter_key, 4)
    column_keys = jax.random.split(pick_key, CB)
    picked_rows = jax.vmap(lambda subkey: jax.random.permutation(subkey, RB)[:RB // 2])(column_keys)
    row_list = picked_rows.reshape(-1).astype(jnp.int32)
    column_list = jnp.repeat(jnp.arange(CB, dtype=jnp.int32), RB // 2)
    shuffle = jax.random.permutation(shuffle_key, KEPT)
    row_list = row_list[shuffle]
    column_list = column_list[shuffle]
    owner_total = SLOTS // CAP
    full_owner = jax.random.randint(owner_key, (), 0, owner_total)
    spread = jax.random.permutation(spread_key, (owner_total - 1) * CAP)
    inverse = jnp.argsort(spread).astype(jnp.int32)
    slot_ids = jnp.arange(SLOTS, dtype=jnp.int32)
    owners = slot_ids // CAP
    other_position = slot_ids - jnp.where(owners > full_owner, CAP, 0)
    other_rank = inverse[jnp.clip(other_position, 0, (owner_total - 1) * CAP - 1)]
    tile_index = jnp.where(owners == full_owner, slot_ids % CAP, CAP + other_rank)
    occupied = tile_index < KEPT
    safe_index = jnp.clip(tile_index, 0, KEPT - 1)
    slot_rows = jnp.where(occupied, row_list[safe_index], -1)
    slot_columns = jnp.where(occupied, column_list[safe_index], -1)
    return (slot_rows.astype(jnp.int32), slot_columns.astype(jnp.int32))


def tile_layout(key):
    base_key = jax.random.fold_in(key, 11)
    quarter_keys = jax.vmap(lambda index: jax.random.fold_in(base_key, index))(jnp.arange(QUARTERS))
    return jax.vmap(quarter_layout)(quarter_keys)


def draw_tile_rows(key, part):
    return tile_layout(key)[0]


def draw_tile_columns(key, part):
    return tile_layout(key)[1]


def shard_levels(rng, shape, shards, least, top_value):
    def one(position, blocks):
        draws = jax.random.uniform(jax.random.fold_in(jax.random.fold_in(rng, 6), position), (blocks,), jnp.float32, least / len(shards), top_value / len(shards))
        return jnp.repeat(jnp.exp(draws), shape[position] // blocks).reshape((-1,) + (1,) * (len(shape) - position - 1))

    factor_of = one(*shards[0])
    for cut in shards[1:]:
        factor_of = factor_of * one(*cut)
    return factor_of


def gaussian(key, extent, scale, reach, pieces=(), kind=jnp.bfloat16):
    entries = scale * jax.random.normal(key, extent, jnp.float32)
    if pieces:
        entries = entries * shard_levels(key, extent, pieces, -0.22, 0.18)
    return jnp.clip(entries, -reach, reach).astype(kind)


def setup_inputs(seed: int = 0) -> dict:
    arg_keys = jax.random.split(jax.random.key(seed), 6)
    normed = draw_normed(jax.random.fold_in(arg_keys[5], 71), 0)
    tile_values = gaussian(arg_keys[1], (QUARTERS, SLOTS, TILE, TILE), (D // 2) ** -0.5, 0.09375, ((0, 4), (1, 64)))
    tile_rows = draw_tile_rows(jax.random.fold_in(arg_keys[5], 71), 0)
    tile_columns = draw_tile_columns(jax.random.fold_in(arg_keys[5], 71), 0)
    cotangent = draw_cotangent(jax.random.fold_in(arg_keys[5], 71), 0)
    return {"normed": normed, "tile_values": tile_values, "tile_rows": tile_rows, "tile_columns": tile_columns, "cotangent": cotangent}


def reference(normed, tile_values, tile_rows, tile_columns, cotangent):
    occupied = tile_columns >= 0
    global_rows = jnp.arange(QUARTERS, dtype=jnp.int32)[:, None] * RB + jnp.maximum(tile_rows, 0)
    pair_index = (global_rows * CB + jnp.maximum(tile_columns, 0)).reshape(-1)
    masked = jnp.where(occupied[:, :, None, None], tile_values.astype(jnp.float32), 0.0).reshape(-1, TILE, TILE)
    blocks = jnp.zeros((D // TILE * CB, TILE, TILE), jnp.float32).at[pair_index].add(masked)
    weight = blocks.reshape(D // TILE, CB, TILE, TILE).transpose(0, 2, 1, 3).reshape(D, KVW).astype(jnp.bfloat16)
    values = jnp.dot(normed, weight, preferred_element_type=jnp.float32).astype(jnp.bfloat16)
    grad_input = jnp.dot(cotangent, weight.T, preferred_element_type=jnp.float32).astype(jnp.bfloat16)
    gradient = jnp.dot(normed.T, cotangent, preferred_element_type=jnp.float32)
    grad_blocks = gradient.reshape(D // TILE, TILE, CB, TILE).transpose(0, 2, 1, 3).reshape(-1, TILE, TILE)
    picked = jnp.where(occupied.reshape(-1)[:, None, None], jnp.take(grad_blocks, pair_index, axis=0), 0.0)
    inverse_rms = lax.rsqrt(lax.optimization_barrier(jnp.mean(picked * picked, axis=(1, 2), keepdims=True)) + 1e-06)
    tile_update = (picked * inverse_rms).astype(jnp.bfloat16).reshape(QUARTERS, SLOTS, TILE, TILE)
    return (values, grad_input, tile_update)
```

```python
import functools

import jax
import jax.numpy as jnp
from jax import lax
from jax.experimental import pallas as pl
from jax.experimental.pallas import tpu as pltpu
from jax.sharding import PartitionSpec as P

MESH = pl.DeviceIdType.MESH
TILE = 128
RING = 4


def rem(value, by):
    return lax.rem(value, jnp.int32(by))


def div(value, by):
    return lax.div(value, jnp.int32(by))


def rows(start, size, unit=16):
    return pl.ds(pl.multiple_of(start, unit), size)


def kernel(
    norm_hbm, cot_hbm, tiles_hbm, places_hbm, values_ref, gi_hbm, update_ref,
    norm, cot, cot_t, tiles, places, table, table_s, weight, part, z1, z2, grad, packed, core_in,
    b1, b2, a1, a2, zl_in, gi, local_sem, send_sem, recv_sem,
):
    tokens, features = norm.shape
    half = tokens // 2
    f, t = lax.axis_index("fsdp"), lax.axis_index("tensor")
    core, y, x, zl = rem(f, 2), rem(div(f, 2), 4), rem(div(f, 8), 4), div(f, 32)
    a = x + core * (y - x)
    b = y + core * (x - y)
    step_a, step_b = 8 - 6 * core, 2 + 6 * core

    def at(aa, bb, zz):
        return (zz * 32 + aa * step_a + bb * step_b + core, t)

    def near(i, by):
        return rem(i + by + RING, RING)

    right, left = (f, near(t, 1)), (f, near(t, -1))
    up_a, down_a = at(near(a, 1), b, zl), at(near(a, -1), b, zl)
    up_b, down_b = at(a, near(b, 1), zl), at(a, near(b, -1), zl)
    other_zl = at(a, b, 1 - zl)
    other_core = (f + 1 - 2 * core, t)

    count = [0]
    started = []

    def send(src, dst, to):
        i = count[0]
        count[0] += 1
        copy = pltpu.make_async_remote_copy(
            src_ref=src, dst_ref=dst, send_sem=send_sem.at[i], recv_sem=recv_sem.at[i],
            device_id=to, device_id_type=MESH,
        )
        started.append(copy)
        return copy

    get_norm = pltpu.make_async_copy(norm_hbm, norm, local_sem.at[0])
    get_norm.start()
    get_cot = pltpu.make_async_copy(cot_hbm, cot.at[t], local_sem.at[1])
    get_cot.start()
    mine = ((core * RING + b) * RING + a) * 2 + zl
    get_tiles = pltpu.make_async_copy(tiles_hbm, tiles.at[pl.ds(mine * 2, 2)], local_sem.at[2])
    get_tiles.start()
    get_places = pltpu.make_async_copy(places_hbm, places.at[pl.ds(mine, 1)], local_sem.at[5])
    get_places.start()

    barrier = pltpu.get_barrier_semaphore()
    partners = (right, left, up_a, down_a, up_b, down_b, other_zl, other_core)
    for partner in partners:
        pl.semaphore_signal(barrier, inc=1, device_id=partner, device_id_type=MESH)
    pl.semaphore_wait(barrier, len(partners))

    first = (
        send(tiles_hbm, tiles.at[pl.ds(mine * 2, 2)], other_zl),
        send(places_hbm, places.at[pl.ds(mine, 1)], other_zl),
    )
    for copy in first:
        copy.start()
    low, high = pl.ds(0, half), pl.ds(half, half)
    cot_r = [send(cot_hbm.at[h], cot.at[t, h], right) for h in (low, high)]
    cot_l = [send(cot_hbm.at[h], cot.at[t, h], left) for h in (high, low)]
    for i in range(2):
        cot_r[i].start()
        cot_l[i].start()
    get_tiles.wait()
    get_places.wait()
    for copy in first:
        copy.wait_recv()

    def send_owners(start, size, to):
        pieces = tiles.at[pl.ds(start * 2, size * 2)], places.at[pl.ds(start, size)]
        copies = [send(piece, piece, to) for piece in pieces]
        for copy in copies:
            copy.start()
        return copies

    def arrived(copies):
        for copy in copies:
            copy.wait_recv()

    def ring_gather(origin, size, index, up, down):
        def block(i):
            return origin + i * size

        ups = send_owners(block(index), size, up)
        downs = send_owners(block(index), size, down)
        yield
        arrived(ups)
        ups = send_owners(block(near(index, -1)), size // 2, up)
        arrived(downs)
        downs = send_owners(block(near(index, 1)) + size // 2, size // 2, down)
        yield
        arrived(ups)
        arrived(downs)
        yield

    for _ in ring_gather((core * RING + b) * 8, 2, a, up_a, down_a):
        pass

    def to_core(i):
        return send_owners((core * RING + i) * 8, 8, other_core)

    second = ring_gather(core * RING * 8, 8, b, up_b, down_b)
    next(second)
    across = to_core(b)
    cot_r[0].wait_recv()
    left_t, right_t = near(t, -1), near(t, 1)
    pass_r = send(cot.at[left_t, low], cot.at[left_t, low], right)
    pass_r.start()
    cot_l[0].wait_recv()
    pass_l = send(cot.at[right_t, high], cot.at[right_t, high], left)
    pass_l.start()
    next(second)
    across += to_core(near(b, -1)) + to_core(near(b, 1))
    next(second)
    across += to_core(near(b, 2))
    arrived(across)

    lane = lax.broadcasted_iota(jnp.int32, (8, TILE), 1)
    slot = lax.broadcasted_iota(jnp.int32, (8, TILE), 0) // 4

    def place(d, sums):
        pair = places[d]
        where_is = jnp.where(pair == lane, d * 2 + slot + 1, 0)
        pair_of = jnp.where(lane == d * 2 + slot, pair, 0)
        return jnp.maximum(sums[0], where_is), sums[1] + pair_of

    zero = jnp.zeros((8, TILE), jnp.int32)
    where_is, pair_of = lax.fori_loop(0, 64, place, (zero, zero))
    table[0:8, :] = where_is
    table[8:16, :] = pair_of
    get_table = pltpu.make_async_copy(table, table_s, local_sem.at[3])
    get_table.start()
    get_table.wait()

    def assemble(r, _):
        for c in range(8):
            code = jnp.maximum(table_s[0, r * 8 + c], table_s[4, r * 8 + c])
            tile = tiles[jnp.maximum(code, 1) - 1]
            tile = jnp.where(code > 0, tile, jnp.zeros_like(tile))
            weight[c // 2, rows(r * TILE, TILE, TILE), (c % 2) * TILE : (c % 2 + 1) * TILE] = tile
        return 0

    lax.fori_loop(0, features // TILE, assemble, 0)
    get_norm.wait()

    def partial(rel, h):
        at_rows = rows(h * half, half, half)
        part[rel, at_rows, :] = jnp.dot(
            norm[at_rows, :], weight[rem(t + rel, RING)], preferred_element_type=jnp.float32
        )

    r1 = send(part.at[2, low], z1.at[0], right)
    l1 = send(part.at[2, high], z1.at[1], left)
    r2 = send(part.at[1, high], z2.at[0, high], right)
    l2 = send(part.at[3, low], z2.at[1, low], left)

    def opposite(h, _):
        partial(2, h)
        pl.when(h == 0)(r1.start)
        pl.when(h == 1)(l1.start)
        return 0

    lax.fori_loop(0, 2, opposite, 0)

    def alone(i, _):
        partial(1 + 2 * i, 1 - i)
        pl.when(i == 0)(r2.start)
        pl.when(i == 1)(l2.start)
        return 0

    lax.fori_loop(0, 2, alone, 0)

    def joined(i, _):
        partial(1 + 2 * i, i)
        return 0

    lax.fori_loop(0, 2, joined, 0)

    def own(h, _):
        partial(0, h)
        return 0

    lax.fori_loop(0, 2, own, 0)

    get_cot.wait()
    cot_r[1].wait_recv()
    cot_l[1].wait_recv()
    pass_r.wait_recv()
    pass_l.wait_recv()
    width = cot.shape[2]
    for q in range(RING):
        cot_t[q * width : (q + 1) * width, :] = cot[q].T

    def gradient(n, _):
        block, side = div(n, 2), rem(n, 2)
        out = jnp.dot(
            cot_t[rows(side * 512, 512, 512), :],
            norm[:, rows(block * 256, 256, 256)],
            preferred_element_type=jnp.float32,
        )
        for i in range(2):
            for j in range(4):
                grad[(block * 2 + i) * 8 + side * 4 + j] = out[
                    j * TILE : (j + 1) * TILE, i * TILE : (i + 1) * TILE
                ]
        return 0

    lax.fori_loop(0, features // 128, gradient, 0)

    def pack(side, whose, i):
        def one(s, _):
            slot = i * 16 + s
            pair = table_s[8, whose * 64 + slot] + table_s[12, whose * 64 + slot]
            tile = grad[jnp.maximum(pair, 0)]
            packed[side, slot] = jnp.where(pair >= 0, tile, jnp.zeros_like(tile))
            return 0

        lax.fori_loop(0, 16, one, 0)

    core_copies = []
    for i in range(RING):
        pack(1, 1 - core, i)
        piece = pl.ds(i * 16, 16)
        copy = send(packed.at[1, piece], core_in.at[piece], other_core)
        copy.start()
        core_copies.append(copy)
    for i in range(RING):
        pack(0, core, i)

    def input_block(n, _):
        th, block = div(n, 8), rem(n, 8)
        at_rows = rows(th * half, half, half)
        at_cols = rows(block * 256, 256, 256)
        lhs = jnp.concatenate([cot[q, at_rows, :] for q in range(RING)], axis=1)
        rhs = jnp.concatenate([weight[q, at_cols, :] for q in range(RING)], axis=1)
        out = lax.dot_general(lhs, rhs, (((1,), (1,)), ((), ())), preferred_element_type=jnp.float32)
        gi[at_rows, at_cols] = out.astype(jnp.bfloat16)
        return 0

    lax.fori_loop(0, 16, input_block, 0)
    put_gi = pltpu.make_async_copy(gi, gi_hbm, local_sem.at[4])
    put_gi.start()

    for copy in core_copies:
        copy.wait_recv()

    def add_core(s, _):
        packed[0, s] = packed[0, s] + core_in[s]
        return 0

    lax.fori_loop(0, 64, add_core, 0)

    def add_into(dst, dst_at, src, src_at, size):
        def one(s, _):
            dst[dst_at + s] = dst[dst_at + s] + src[src_at + s]
            return 0

        lax.fori_loop(0, size, one, 0)

    acc = packed.at[0]

    def ring_scatter(size, origin, index, up, down, in1, in2):
        part_size = size // 2

        def block(i):
            return origin + i * size

        far = block(near(index, 2))
        above, below = block(near(index, 1)), block(near(index, -1))
        firsts, lasts = pl.ds(0, part_size), pl.ds(part_size, part_size)
        u1 = send(acc.at[pl.ds(far, part_size)], in1.at[firsts], up)
        d1 = send(acc.at[pl.ds(far + part_size, part_size)], in1.at[lasts], down)
        u1.start()
        d1.start()
        u2 = send(acc.at[pl.ds(above + part_size, part_size)], in2.at[0, lasts], up)
        d2 = send(acc.at[pl.ds(below, part_size)], in2.at[1, firsts], down)
        u2.start()
        d2.start()
        yield
        u1.wait_recv()
        add_into(acc, above, in1, 0, part_size)
        u3 = send(acc.at[pl.ds(above, part_size)], in2.at[0, firsts], up)
        u3.start()
        d1.wait_recv()
        add_into(acc, below + part_size, in1, part_size, part_size)
        d3 = send(acc.at[pl.ds(below + part_size, part_size)], in2.at[1, lasts], down)
        d3.start()
        yield
        for copy in (u2, d2, u3, d3):
            copy.wait_recv()
        keep = block(index)

        def one(s, _):
            acc[keep + s] = acc[keep + s] + in2[0, s] + in2[1, s]
            return 0

        lax.fori_loop(0, size, one, 0)
        yield

    over_b = ring_scatter(16, 0, b, up_b, down_b, b1, b2)
    next(over_b)

    quarter = half // 2
    lasts_r, lasts_l = [], []
    r1.wait_recv()
    for i in range(2):
        piece = pl.ds(i * quarter, quarter)
        part[1, piece, :] = part[1, piece, :] + z1[0, piece, :]
        copy = send(part.at[1, piece], z2.at[0, piece], right)
        copy.start()
        lasts_r.append(copy)
    l1.wait_recv()
    for i in range(2):
        piece = pl.ds(half + i * quarter, quarter)
        part[3, piece, :] = part[3, piece, :] + z1[1, pl.ds(i * quarter, quarter), :]
        copy = send(part.at[3, piece], z2.at[1, piece], left)
        copy.start()
        lasts_l.append(copy)

    next(over_b)
    next(over_b)
    over_a = ring_scatter(4, b * 16, a, up_a, down_a, a1, a2)
    for _ in over_a:
        pass
    kept = b * 16 + a * 4
    zl_copy = send(acc.at[pl.ds(kept + 2 * (1 - zl), 2)], zl_in, other_zl)
    zl_copy.start()

    def finish(i):
        piece = pl.ds(i * quarter, quarter)
        values_ref[piece, :] = (part[0, piece, :] + z2[0, piece, :] + z2[1, piece, :]).astype(jnp.bfloat16)

    zl_copy.wait_recv()
    for k in range(2):
        tile = acc[kept + 2 * zl + k] + zl_in[k]
        mean = jnp.sum(tile * tile, axis=(0, 1), keepdims=True) / (TILE * TILE)
        update_ref[k] = (tile * lax.rsqrt(mean + 1e-06)).T.astype(jnp.bfloat16)

    r2.wait_recv()
    l2.wait_recv()
    for i in range(2):
        lasts_r[i].wait_recv()
        finish(i)
        lasts_l[i].wait_recv()
        finish(2 + i)
    put_gi.wait()
    for copy in started:
        copy.wait_send()


COPIES = 57


def local(normed, tile_values, tile_rows, tile_columns, cotangent):
    tokens, features = normed.shape
    width = cotangent.shape[1]
    pair = jnp.where(tile_columns >= 0, tile_rows * 8 + tile_columns, -1)
    places = jnp.broadcast_to(pair.reshape(2, 1, 1), (2, 4, TILE)).reshape(1, 8, TILE)
    anywhere = pl.BlockSpec(memory_space=pl.ANY)
    vmem = pl.BlockSpec(memory_space=pltpu.VMEM)
    f32, bf16 = jnp.float32, jnp.bfloat16
    values, grad_input, update = pl.pallas_call(
        kernel,
        out_shape=(
            jax.ShapeDtypeStruct((tokens, width), bf16),
            jax.ShapeDtypeStruct((tokens, features), bf16),
            jax.ShapeDtypeStruct((2, TILE, TILE), bf16),
        ),
        in_specs=[anywhere] * 4,
        out_specs=(vmem, anywhere, vmem),
        scratch_shapes=[
            pltpu.VMEM((tokens, features), bf16),
            pltpu.VMEM((RING, tokens, width), bf16),
            pltpu.VMEM((RING * width, tokens), bf16),
            pltpu.VMEM((128, TILE, TILE), bf16),
            pltpu.VMEM((64, 8, TILE), jnp.int32),
            pltpu.VMEM((16, TILE), jnp.int32),
            pltpu.SMEM((16, TILE), jnp.int32),
            pltpu.VMEM((RING, features, width), bf16),
            pltpu.VMEM((RING, tokens, width), f32),
            pltpu.VMEM((2, tokens // 2, width), f32),
            pltpu.VMEM((2, tokens, width), f32),
            pltpu.VMEM((128, TILE, TILE), f32),
            pltpu.VMEM((2, 64, TILE, TILE), f32),
            pltpu.VMEM((64, TILE, TILE), f32),
            pltpu.VMEM((16, TILE, TILE), f32),
            pltpu.VMEM((2, 16, TILE, TILE), f32),
            pltpu.VMEM((4, TILE, TILE), f32),
            pltpu.VMEM((2, 4, TILE, TILE), f32),
            pltpu.VMEM((2, TILE, TILE), f32),
            pltpu.VMEM((tokens, features), bf16),
            pltpu.SemaphoreType.DMA((6,)),
            pltpu.SemaphoreType.DMA((COPIES,)),
            pltpu.SemaphoreType.DMA((COPIES,)),
        ],
        compiler_params=pltpu.CompilerParams(
            collective_id=0, has_side_effects=True, vmem_limit_bytes=67043328
        ),
    )(normed, cotangent, tile_values.reshape(2, TILE, TILE), places)
    return values, grad_input, update[None]


def solution(mesh):
    in_specs = (
        P("fsdp", "tensor"),
        P("tensor", "fsdp", None, None),
        P("tensor", "fsdp"),
        P("tensor", "fsdp"),
        P("fsdp", "tensor"),
    )
    out_specs = (P("fsdp", "tensor"), P("fsdp", "tensor"), P("tensor", "fsdp", None, None))
    return jax.shard_map(local, mesh=mesh, in_specs=in_specs, out_specs=out_specs, check_vma=False)
```

```python
import functools

import jax
import jax.numpy as jnp
from jax import lax
from jax.experimental import pallas as pl
from jax.experimental.pallas import tpu as pltpu
from jax.sharding import PartitionSpec as P

MESH = pl.DeviceIdType.MESH
TILE = 128
RING = 4


def rem(value, by):
    return lax.rem(value, jnp.int32(by))


def div(value, by):
    return lax.div(value, jnp.int32(by))


def rows(start, size, unit=16):
    return pl.ds(pl.multiple_of(start, unit), size)


CODED = True


def encode(x):
    if not CODED:
        return x, None
    groups = x.reshape(8, x.shape[0] // 8, x.shape[1])
    largest = jnp.maximum(jnp.max(jnp.abs(groups), axis=1), 1e-30)
    whole = lax.round(groups * (32767.0 / largest)[:, None, :], lax.RoundingMethod.TO_NEAREST_EVEN)
    return whole.astype(jnp.int32).astype(jnp.int16).reshape(x.shape), largest * (1 / 32767.0)


def decode(coded, scales):
    if not CODED:
        return coded
    groups = coded.astype(jnp.int32).astype(jnp.float32).reshape(8, coded.shape[0] // 8, coded.shape[1])
    return (groups * scales[:, None, :]).reshape(coded.shape)


def kernel(
    norm_hbm, cot_hbm, tiles_hbm, places_hbm, values_ref, gi_hbm, update_ref,
    norm, cot, cot_t, tiles, places, table, table_s, weight, own, joint, z_out, z_in, s_out, s_in,
    grad, packed, core_in, b1, b2, a1, a2, zl_in, gi, local_sem, send_sem, recv_sem,
    z_send, z_recv, s_send, s_recv,
):
    tokens, features = norm.shape
    half = tokens // 2
    f, t = lax.axis_index("fsdp"), lax.axis_index("tensor")
    core, y, x, zl = rem(f, 2), rem(div(f, 2), 4), rem(div(f, 8), 4), div(f, 32)
    a = x + core * (y - x)
    b = y + core * (x - y)
    step_a, step_b = 8 - 6 * core, 2 + 6 * core

    def at(aa, bb, zz):
        return (zz * 32 + aa * step_a + bb * step_b + core, t)

    def near(i, by):
        return rem(i + by + RING, RING)

    right, left = (f, near(t, 1)), (f, near(t, -1))
    up_a, down_a = at(near(a, 1), b, zl), at(near(a, -1), b, zl)
    up_b, down_b = at(a, near(b, 1), zl), at(a, near(b, -1), zl)
    other_zl = at(a, b, 1 - zl)
    other_core = (f + 1 - 2 * core, t)

    count = [0]
    started = []

    def send(src, dst, to):
        i = count[0]
        count[0] += 1
        copy = pltpu.make_async_remote_copy(
            src_ref=src, dst_ref=dst, send_sem=send_sem.at[i], recv_sem=recv_sem.at[i],
            device_id=to, device_id_type=MESH,
        )
        started.append(copy)
        return copy

    get_norm = pltpu.make_async_copy(norm_hbm, norm, local_sem.at[0])
    get_norm.start()
    get_cot = pltpu.make_async_copy(cot_hbm, cot.at[t], local_sem.at[1])
    get_cot.start()
    mine = ((core * RING + b) * RING + a) * 2 + zl
    get_tiles = pltpu.make_async_copy(tiles_hbm, tiles.at[pl.ds(mine * 2, 2)], local_sem.at[2])
    get_tiles.start()
    get_places = pltpu.make_async_copy(places_hbm, places.at[pl.ds(mine, 1)], local_sem.at[5])
    get_places.start()

    barrier = pltpu.get_barrier_semaphore()
    partners = (right, left, up_a, down_a, up_b, down_b, other_zl, other_core)
    for partner in partners:
        pl.semaphore_signal(barrier, inc=1, device_id=partner, device_id_type=MESH)
    pl.semaphore_wait(barrier, len(partners))

    first = (
        send(tiles_hbm, tiles.at[pl.ds(mine * 2, 2)], other_zl),
        send(places_hbm, places.at[pl.ds(mine, 1)], other_zl),
    )
    for copy in first:
        copy.start()
    low, high = pl.ds(0, half), pl.ds(half, half)
    cot_r = [send(cot_hbm.at[h], cot.at[t, h], right) for h in (low, high)]
    cot_l = [send(cot_hbm.at[h], cot.at[t, h], left) for h in (high, low)]
    for copy in first:
        copy.wait_recv()
    for i in range(2):
        cot_r[i].start()
        cot_l[i].start()
    get_tiles.wait()
    get_places.wait()

    def send_owners(start, size, to):
        pieces = tiles.at[pl.ds(start * 2, size * 2)], places.at[pl.ds(start, size)]
        copies = [send(piece, piece, to) for piece in pieces]
        for copy in copies:
            copy.start()
        return copies

    def arrived(copies):
        for copy in copies:
            copy.wait_recv()

    def ring_gather(origin, size, index, up, down):
        def block(i):
            return origin + i * size

        ups = send_owners(block(index), size, up)
        downs = send_owners(block(index), size, down)
        yield
        arrived(ups)
        ups = send_owners(block(near(index, -1)), size // 2, up)
        arrived(downs)
        downs = send_owners(block(near(index, 1)) + size // 2, size // 2, down)
        yield
        arrived(ups)
        arrived(downs)
        yield

    def to_core(i):
        return send_owners((core * RING + i) * 8, 8, other_core)

    def turn(q):
        cot_t[q] = cot[q].T

    def gradient(q, start, stop):
        def one(n, _):
            out = jnp.dot(
                cot_t[q], norm[:, rows(n * 256, 256, 256)], preferred_element_type=jnp.float32
            )
            for i in range(2):
                for j in range(2):
                    grad[(n * 2 + i) * 8 + q * 2 + j] = out[
                        j * TILE : (j + 1) * TILE, i * TILE : (i + 1) * TILE
                    ]
            return 0

        lax.fori_loop(start, stop, one, 0)

    steps = features // 256
    left_t, right_t, far_t = near(t, -1), near(t, 1), near(t, 2)
    first_ring = ring_gather((core * RING + b) * 8, 2, a, up_a, down_a)
    next(first_ring)
    get_cot.wait()
    turn(t)
    next(first_ring)
    get_norm.wait()
    gradient(t, 0, steps // 4)
    next(first_ring)
    second_ring = ring_gather(core * RING * 8, 8, b, up_b, down_b)
    next(second_ring)
    across = to_core(b)
    gradient(t, steps // 4, steps)
    cot_r[0].wait_recv()
    pass_r = send(cot.at[left_t, low], cot.at[left_t, low], right)
    pass_r.start()
    cot_l[0].wait_recv()
    pass_l = send(cot.at[right_t, high], cot.at[right_t, high], left)
    pass_l.start()
    next(second_ring)
    across += to_core(near(b, -1)) + to_core(near(b, 1))
    next(second_ring)
    across += to_core(near(b, 2))
    cot_r[1].wait_recv()
    turn(left_t)
    gradient(left_t, 0, steps)
    cot_l[1].wait_recv()
    turn(right_t)
    gradient(right_t, 0, steps)
    arrived(across)

    lane = lax.broadcasted_iota(jnp.int32, (8, TILE), 1)
    slot = lax.broadcasted_iota(jnp.int32, (8, TILE), 0) // 4

    def place(d, sums):
        pair = places[d]
        where_is = jnp.where(pair == lane, d * 2 + slot + 1, 0)
        pair_of = jnp.where(lane == d * 2 + slot, pair, 0)
        return jnp.maximum(sums[0], where_is), sums[1] + pair_of

    zero = jnp.zeros((8, TILE), jnp.int32)
    where_is, pair_of = lax.fori_loop(0, 64, place, (zero, zero))
    table[0:8, :] = where_is
    table[8:16, :] = pair_of
    get_table = pltpu.make_async_copy(table, table_s, local_sem.at[6])
    get_table.start()
    get_table.wait()

    def assemble(r, _):
        for c in range(8):
            code = jnp.maximum(table_s[0, r * 8 + c], table_s[4, r * 8 + c])
            tile = tiles[jnp.maximum(code, 1) - 1]
            tile = jnp.where(code > 0, tile, jnp.zeros_like(tile))
            weight[c // 2, rows(r * TILE, TILE, TILE), (c % 2) * TILE : (c % 2 + 1) * TILE] = tile
        return 0

    lax.fori_loop(0, features // TILE, assemble, 0)

    chunk = tokens // 4

    def partial(rel, c):
        return jnp.dot(
            norm[rows(c * chunk, chunk, chunk), :],
            weight[rem(t + rel, RING)],
            preferred_element_type=jnp.float32,
        )

    def message(way, j):
        to = (f, rem(t + 1 + 2 * way, RING))
        copies = [
            pltpu.make_async_remote_copy(
                src_ref=z_out.at[way, j], dst_ref=z_in.at[way, j], send_sem=z_send.at[way, j],
                recv_sem=z_recv.at[way, j], device_id=to, device_id_type=MESH,
            )
        ]
        if CODED:
            copies += [
                pltpu.make_async_remote_copy(
                    src_ref=s_out.at[way, j], dst_ref=s_in.at[way, j], send_sem=s_send.at[way, j],
                    recv_sem=s_recv.at[way, j], device_id=to, device_id_type=MESH,
                )
            ]
        return copies

    def post(way, j, x):
        coded, scales = encode(x)
        z_out[way, j] = coded
        if CODED:
            s_out[way, j] = scales
        for copy in message(way, j):
            copy.start()

    def received(way, j):
        return decode(z_in[way, j], s_in[way, j])

    def to_far(i, _):
        way, j = div(i, 2), rem(i, 2)
        post(way, j, partial(2, i))
        return 0

    lax.fori_loop(0, 4, to_far, 0)

    def to_near(i, _):
        way, j = div(i, 2), rem(i, 2)
        post(way, 2 + j, partial(1 + 2 * way, (1 - way) * 2 + j))
        return 0

    lax.fori_loop(0, 4, to_near, 0)

    arrived([pass_r, pass_l])
    turn(far_t)
    gradient(far_t, 0, steps)

    def pack(side, whose, i):
        def one(s, _):
            slot = i * 16 + s
            pair = table_s[8, whose * 64 + slot] + table_s[12, whose * 64 + slot]
            tile = grad[jnp.maximum(pair, 0)]
            packed[side, slot] = jnp.where(pair >= 0, tile, jnp.zeros_like(tile))
            return 0

        lax.fori_loop(0, 16, one, 0)

    core_copies = []
    for by in (2, 1, -1, 0):
        i = near(a, by)
        pack(1, 1 - core, i)
        piece = pl.ds(i * 16, 16)
        copy = send(packed.at[1, piece], core_in.at[piece], other_core)
        copy.start()
        core_copies.append(copy)
    for i in range(RING):
        pack(0, core, i)

    def rest(i, _):
        joint[i] = partial(1 + 2 * div(i, 2), i)
        own[i] = partial(0, i)
        return 0

    lax.fori_loop(0, 4, rest, 0)

    def input_block(n, _):
        th, block = div(n, 8), rem(n, 8)
        at_rows = rows(th * half, half, half)
        at_cols = rows(block * 256, 256, 256)
        lhs = jnp.concatenate([cot[q, at_rows, :] for q in range(RING)], axis=1)
        rhs = jnp.concatenate([weight[q, at_cols, :] for q in range(RING)], axis=1)
        out = lax.dot_general(lhs, rhs, (((1,), (1,)), ((), ())), preferred_element_type=jnp.float32)
        gi[at_rows, at_cols] = out.astype(jnp.bfloat16)
        return 0

    def grad_input(th):
        lax.fori_loop(th * 8, th * 8 + 8, input_block, 0)
        at_rows = pl.ds(th * half, half)
        put = pltpu.make_async_copy(gi.at[at_rows], gi_hbm.at[at_rows], local_sem.at[3 + th])
        put.start()
        return put

    def add_into(dst, dst_at, src, src_at, size):
        def one(s, _):
            dst[dst_at + s] = dst[dst_at + s] + src[src_at + s]
            return 0

        lax.fori_loop(0, size, one, 0)

    acc = packed.at[0]

    def ring_scatter(size, origin, index, up, down, in1, in2, before):
        part_size = size // 2

        def block(i):
            return origin + i * size

        far = block(near(index, 2))
        above, below = block(near(index, 1)), block(near(index, -1))
        firsts, lasts = pl.ds(0, part_size), pl.ds(part_size, part_size)
        before(2)
        u1 = send(acc.at[pl.ds(far, part_size)], in1.at[firsts], up)
        d1 = send(acc.at[pl.ds(far + part_size, part_size)], in1.at[lasts], down)
        u1.start()
        d1.start()
        before(1)
        before(-1)
        u2 = send(acc.at[pl.ds(above + part_size, part_size)], in2.at[0, lasts], up)
        d2 = send(acc.at[pl.ds(below, part_size)], in2.at[1, firsts], down)
        u2.start()
        d2.start()
        before(0)
        yield
        u1.wait_recv()
        add_into(acc, above, in1, 0, part_size)
        u3 = send(acc.at[pl.ds(above, part_size)], in2.at[0, firsts], up)
        u3.start()
        d1.wait_recv()
        add_into(acc, below + part_size, in1, part_size, part_size)
        d3 = send(acc.at[pl.ds(below + part_size, part_size)], in2.at[1, lasts], down)
        d3.start()
        yield
        for copy in (u2, d2, u3, d3):
            copy.wait_recv()
        keep = block(index)

        def one(s, _):
            acc[keep + s] = acc[keep + s] + in2[0, s] + in2[1, s]
            return 0

        lax.fori_loop(0, size, one, 0)
        yield

    def add_core(by):
        core_copies[(2, 1, -1, 0).index(by)].wait_recv()
        start = near(b, by) * 16
        add_into(acc, start, core_in, start, 16)

    over_b = ring_scatter(16, 0, b, up_b, down_b, b1, b2, add_core)
    next(over_b)

    def pass_on(i, _):
        way, j = div(i, 2), rem(i, 2)
        for copy in message(way, j):
            copy.wait_recv()
        post(way, 4 + j, joint[i] + received(way, j))
        return 0

    lax.fori_loop(0, 4, pass_on, 0)
    puts = [grad_input(0)]
    next(over_b)
    puts += [grad_input(1)]
    next(over_b)
    for _ in ring_scatter(4, b * 16, a, up_a, down_a, a1, a2, lambda by: None):
        pass
    kept = b * 16 + a * 4
    zl_copy = send(acc.at[pl.ds(kept + 2 * (1 - zl), 2)], zl_in, other_zl)
    zl_copy.start()

    def finish(i, _):
        h, j = div(i, 2), rem(i, 2)
        from_left, from_right = 4 - 2 * h + j, 2 + 2 * h + j
        for copy in message(0, from_left) + message(1, from_right):
            copy.wait_recv()
        total = own[i] + received(0, from_left) + received(1, from_right)
        values_ref[rows(i * chunk, chunk, chunk), :] = total.astype(jnp.bfloat16)
        return 0

    lax.fori_loop(0, 4, finish, 0)
    zl_copy.wait_recv()
    for k in range(2):
        tile = acc[kept + 2 * zl + k] + zl_in[k]
        mean = jnp.sum(tile * tile, axis=(0, 1), keepdims=True) / (TILE * TILE)
        update_ref[k] = (tile * lax.rsqrt(mean + 1e-06)).T.astype(jnp.bfloat16)
    for put in puts:
        put.wait()
    for copy in started:
        copy.wait_send()
    for way in range(2):
        for j in range(6):
            for copy in message(way, j):
                copy.wait_send()


COPIES = 49


def local(normed, tile_values, tile_rows, tile_columns, cotangent):
    tokens, features = normed.shape
    width = cotangent.shape[1]
    pair = jnp.where(tile_columns >= 0, tile_rows * 8 + tile_columns, -1)
    places = jnp.broadcast_to(pair.reshape(2, 1, 1), (2, 4, TILE)).reshape(1, 8, TILE)
    anywhere = pl.BlockSpec(memory_space=pl.ANY)
    vmem = pl.BlockSpec(memory_space=pltpu.VMEM)
    f32, bf16 = jnp.float32, jnp.bfloat16
    sent = jnp.int16 if CODED else f32
    values, grad_input, update = pl.pallas_call(
        kernel,
        out_shape=(
            jax.ShapeDtypeStruct((tokens, width), bf16),
            jax.ShapeDtypeStruct((tokens, features), bf16),
            jax.ShapeDtypeStruct((2, TILE, TILE), bf16),
        ),
        in_specs=[anywhere] * 4,
        out_specs=(vmem, anywhere, vmem),
        scratch_shapes=[
            pltpu.VMEM((tokens, features), bf16),
            pltpu.VMEM((RING, tokens, width), bf16),
            pltpu.VMEM((RING, width, tokens), bf16),
            pltpu.VMEM((128, TILE, TILE), bf16),
            pltpu.VMEM((64, 8, TILE), jnp.int32),
            pltpu.VMEM((16, TILE), jnp.int32),
            pltpu.SMEM((16, TILE), jnp.int32),
            pltpu.VMEM((RING, features, width), bf16),
            pltpu.VMEM((4, tokens // 4, width), f32),
            pltpu.VMEM((4, tokens // 4, width), f32),
            pltpu.VMEM((2, 6, tokens // 4, width), sent),
            pltpu.VMEM((2, 6, tokens // 4, width), sent),
            pltpu.VMEM((2, 6, 8, width), f32),
            pltpu.VMEM((2, 6, 8, width), f32),
            pltpu.VMEM((128, TILE, TILE), f32),
            pltpu.VMEM((2, 64, TILE, TILE), f32),
            pltpu.VMEM((64, TILE, TILE), f32),
            pltpu.VMEM((16, TILE, TILE), f32),
            pltpu.VMEM((2, 16, TILE, TILE), f32),
            pltpu.VMEM((4, TILE, TILE), f32),
            pltpu.VMEM((2, 4, TILE, TILE), f32),
            pltpu.VMEM((2, TILE, TILE), f32),
            pltpu.VMEM((tokens, features), bf16),
            pltpu.SemaphoreType.DMA((7,)),
            pltpu.SemaphoreType.DMA((COPIES,)),
            pltpu.SemaphoreType.DMA((COPIES,)),
            *[pltpu.SemaphoreType.DMA((2, 6))] * 4,
        ],
        compiler_params=pltpu.CompilerParams(
            collective_id=0, has_side_effects=True, vmem_limit_bytes=67043328
        ),
    )(normed, cotangent, tile_values.reshape(2, TILE, TILE), places)
    return values, grad_input, update[None]


def solution(mesh):
    in_specs = (
        P("fsdp", "tensor"),
        P("tensor", "fsdp", None, None),
        P("tensor", "fsdp"),
        P("tensor", "fsdp"),
        P("fsdp", "tensor"),
    )
    out_specs = (P("fsdp", "tensor"), P("fsdp", "tensor"), P("tensor", "fsdp", None, None))
    return jax.shard_map(local, mesh=mesh, in_specs=in_specs, out_specs=out_specs, check_vma=False)
```

```python
import functools

import jax
import jax.numpy as jnp
from jax import lax
from jax.experimental import pallas as pl
from jax.experimental.pallas import tpu as pltpu
from jax.sharding import PartitionSpec as P

MESH = pl.DeviceIdType.MESH
TILE = 128
RING = 4


def rem(value, by):
    return lax.rem(value, jnp.int32(by))


def div(value, by):
    return lax.div(value, jnp.int32(by))


def rows(start, size, unit=16):
    return pl.ds(pl.multiple_of(start, unit), size)


def encode(x):
    groups = x.reshape(8, x.shape[0] // 8, x.shape[1])
    largest = jnp.maximum(jnp.max(jnp.abs(groups), axis=1), 1e-30)
    whole = lax.round(groups * (32767.0 / largest)[:, None, :], lax.RoundingMethod.TO_NEAREST_EVEN)
    return whole.astype(jnp.int32).astype(jnp.int16).reshape(x.shape), largest * (1 / 32767.0)


def decode(coded, scales):
    groups = coded.astype(jnp.int32).astype(jnp.float32).reshape(8, coded.shape[0] // 8, coded.shape[1])
    return (groups * scales[:, None, :]).reshape(coded.shape)


def kernel(
    norm_hbm, cot_hbm, tiles_hbm, rows_ref, columns_ref, values_ref, gi_hbm, update_ref,
    norm, cot, cot_t, tiles, places, table, table_s, weight, own, joint, z_out, z_in, s_out, s_in,
    grad, packed, core_in, bq_out, bq_in, br_out, br_in, aq_out, aq_in, ar_out, ar_in, zl_in, gi, local_sem, send_sem, recv_sem,
    z_send, z_recv, s_send, s_recv,
):
    tokens, features = norm.shape
    half = tokens // 2
    f, t = lax.axis_index("fsdp"), lax.axis_index("tensor")
    core, y, x, zl = rem(f, 2), rem(div(f, 2), 4), rem(div(f, 8), 4), div(f, 32)
    a = x + core * (y - x)
    b = y + core * (x - y)
    step_a, step_b = 8 - 6 * core, 2 + 6 * core

    def at(aa, bb, zz):
        return (zz * 32 + aa * step_a + bb * step_b + core, t)

    def near(i, by):
        return rem(i + by + RING, RING)

    right, left = (f, near(t, 1)), (f, near(t, -1))
    up_a, down_a = at(near(a, 1), b, zl), at(near(a, -1), b, zl)
    up_b, down_b = at(a, near(b, 1), zl), at(a, near(b, -1), zl)
    other_zl = at(a, b, 1 - zl)
    other_core = (f + 1 - 2 * core, t)

    count = [0]
    started = []

    def send(src, dst, to):
        i = count[0]
        count[0] += 1
        copy = pltpu.make_async_remote_copy(
            src_ref=src, dst_ref=dst, send_sem=send_sem.at[i], recv_sem=recv_sem.at[i],
            device_id=to, device_id_type=MESH,
        )
        started.append(copy)
        return copy

    get_norm = pltpu.make_async_copy(norm_hbm, norm, local_sem.at[0])
    get_norm.start()
    get_cot = pltpu.make_async_copy(cot_hbm, cot.at[t], local_sem.at[1])
    get_cot.start()
    mine = ((core * RING + b) * RING + a) * 2 + zl
    get_tiles = pltpu.make_async_copy(tiles_hbm, tiles.at[pl.ds(mine * 2, 2)], local_sem.at[2])
    get_tiles.start()
    pairs = [
        jnp.where(columns_ref[0, k] >= 0, rows_ref[0, k] * 8 + columns_ref[0, k], -1) for k in range(2)
    ]
    lane = lax.broadcasted_iota(jnp.int32, (8, TILE), 1)
    slot = lax.broadcasted_iota(jnp.int32, (8, TILE), 0) // 4
    places[mine] = jnp.where(slot == 0, pairs[0], pairs[1])

    barrier = pltpu.get_barrier_semaphore()
    partners = (right, left, up_a, down_a, up_b, down_b, other_zl, other_core)
    for partner in partners:
        pl.semaphore_signal(barrier, inc=1, device_id=partner, device_id_type=MESH)
    pl.semaphore_wait(barrier, len(partners))

    first = (
        send(tiles_hbm, tiles.at[pl.ds(mine * 2, 2)], other_zl),
        send(places.at[mine], places.at[mine], other_zl),
    )
    for copy in first:
        copy.start()
    low, high = pl.ds(0, half), pl.ds(half, half)
    cot_r = [send(cot_hbm.at[h], cot.at[t, h], right) for h in (low, high)]
    cot_l = [send(cot_hbm.at[h], cot.at[t, h], left) for h in (high, low)]
    for copy in first:
        copy.wait_recv()
    for i in range(2):
        cot_r[i].start()
        cot_l[i].start()
    get_tiles.wait()

    def send_owners(start, size, to):
        pieces = tiles.at[pl.ds(start * 2, size * 2)], places.at[pl.ds(start, size)]
        copies = [send(piece, piece, to) for piece in pieces]
        for copy in copies:
            copy.start()
        return copies

    def arrived(copies):
        for copy in copies:
            copy.wait_recv()

    def ring_gather(origin, size, index, up, down):
        def block(i):
            return origin + i * size

        ups = send_owners(block(index), size, up)
        downs = send_owners(block(index), size, down)
        yield
        arrived(ups)
        ups = send_owners(block(near(index, -1)), size // 2, up)
        arrived(downs)
        downs = send_owners(block(near(index, 1)) + size // 2, size // 2, down)
        yield
        arrived(ups)
        arrived(downs)
        yield

    def to_core(i):
        return send_owners((core * RING + i) * 8, 8, other_core)

    def turn(q):
        cot_t[q] = cot[q].T

    def gradient(q, start, stop):
        def one(n, _):
            out = jnp.dot(
                cot_t[q], norm[:, rows(n * 256, 256, 256)], preferred_element_type=jnp.float32
            )
            for i in range(2):
                for j in range(2):
                    grad[(n * 2 + i) * 8 + q * 2 + j] = out[
                        j * TILE : (j + 1) * TILE, i * TILE : (i + 1) * TILE
                    ]
            return 0

        lax.fori_loop(start, stop, one, 0)

    steps = features // 256
    left_t, right_t, far_t = near(t, -1), near(t, 1), near(t, 2)
    first_ring = ring_gather((core * RING + b) * 8, 2, a, up_a, down_a)
    next(first_ring)
    get_cot.wait()
    turn(t)
    next(first_ring)
    get_norm.wait()
    gradient(t, 0, steps // 4)
    next(first_ring)
    second_ring = ring_gather(core * RING * 8, 8, b, up_b, down_b)
    next(second_ring)
    across = to_core(b)
    gradient(t, steps // 4, steps)
    cot_r[0].wait_recv()
    pass_r = send(cot.at[left_t, low], cot.at[left_t, low], right)
    pass_r.start()
    cot_l[0].wait_recv()
    pass_l = send(cot.at[right_t, high], cot.at[right_t, high], left)
    pass_l.start()
    next(second_ring)
    across += to_core(near(b, -1)) + to_core(near(b, 1))
    next(second_ring)
    across += to_core(near(b, 2))
    cot_r[1].wait_recv()
    turn(left_t)
    gradient(left_t, 0, steps)
    cot_l[1].wait_recv()
    turn(right_t)
    gradient(right_t, 0, steps)
    arrived(across)


    def place(d, sums):
        pair = places[d]
        where_is = jnp.where(pair == lane, d * 2 + slot + 1, 0)
        pair_of = jnp.where(lane == d * 2 + slot, pair, 0)
        return jnp.maximum(sums[0], where_is), sums[1] + pair_of

    zero = jnp.zeros((8, TILE), jnp.int32)
    where_is, pair_of = lax.fori_loop(0, 64, place, (zero, zero))
    table[0:8, :] = where_is
    table[8:16, :] = pair_of
    get_table = pltpu.make_async_copy(table, table_s, local_sem.at[6])
    get_table.start()
    get_table.wait()

    def assemble(r, _):
        for c in range(8):
            code = jnp.maximum(table_s[0, r * 8 + c], table_s[4, r * 8 + c])
            tile = tiles[jnp.maximum(code, 1) - 1]
            tile = jnp.where(code > 0, tile, jnp.zeros_like(tile))
            weight[c // 2, rows(r * TILE, TILE, TILE), (c % 2) * TILE : (c % 2 + 1) * TILE] = tile
        return 0

    lax.fori_loop(0, features // TILE, assemble, 0)

    chunk = tokens // 4

    def partial(rel, c):
        return jnp.dot(
            norm[rows(c * chunk, chunk, chunk), :],
            weight[rem(t + rel, RING)],
            preferred_element_type=jnp.float32,
        )

    def message(way, j):
        to = (f, rem(t + 1 + 2 * way, RING))
        copies = [
            pltpu.make_async_remote_copy(
                src_ref=src.at[way, j], dst_ref=dst.at[way, j], send_sem=send_at.at[way, j],
                recv_sem=recv_at.at[way, j], device_id=to, device_id_type=MESH,
            )
            for src, dst, send_at, recv_at in (
                (z_out, z_in, z_send, z_recv), (s_out, s_in, s_send, s_recv)
            )
        ]
        return copies

    def post(way, j, x):
        z_out[way, j], s_out[way, j] = encode(x)
        for copy in message(way, j):
            copy.start()

    def received(way, j):
        return decode(z_in[way, j], s_in[way, j])

    def to_far(i, _):
        way, j = div(i, 2), rem(i, 2)
        post(way, j, partial(2, i))
        return 0

    lax.fori_loop(0, 4, to_far, 0)

    arrived([pass_r, pass_l])
    turn(far_t)
    gradient(far_t, 0, steps)

    def pack(side, whose, i):
        def one(s, _):
            slot = i * 16 + s
            pair = table_s[8, whose * 64 + slot] + table_s[12, whose * 64 + slot]
            tile = grad[jnp.maximum(pair, 0)]
            packed[side, slot] = jnp.where(pair >= 0, tile, jnp.zeros_like(tile))
            return 0

        lax.fori_loop(0, 16, one, 0)

    core_copies = []
    for by in (2, 1, -1, 0):
        i = near(a, by)
        pack(1, 1 - core, i)
        piece = pl.ds(i * 16, 16)
        copy = send(packed.at[1, piece], core_in.at[piece], other_core)
        copy.start()
        core_copies.append(copy)
    for i in range(RING):
        pack(0, core, i)

    def input_block(n, _):
        th, block = div(n, 8), rem(n, 8)
        at_rows = rows(th * half, half, half)
        at_cols = rows(block * 256, 256, 256)
        lhs = jnp.concatenate([cot[q, at_rows, :] for q in range(RING)], axis=1)
        rhs = jnp.concatenate([weight[q, at_cols, :] for q in range(RING)], axis=1)
        out = lax.dot_general(lhs, rhs, (((1,), (1,)), ((), ())), preferred_element_type=jnp.float32)
        gi[at_rows, at_cols] = out.astype(jnp.bfloat16)
        return 0

    def grad_input(th):
        lax.fori_loop(th * 8, th * 8 + 8, input_block, 0)
        at_rows = pl.ds(th * half, half)
        put = pltpu.make_async_copy(gi.at[at_rows], gi_hbm.at[at_rows], local_sem.at[3 + th])
        put.start()
        return put

    def add_into(dst, dst_at, src, src_at, size):
        def one(s, _):
            dst[dst_at + s] = dst[dst_at + s] + src[src_at + s]
            return 0

        lax.fori_loop(0, size, one, 0)

    acc = packed.at[0]

    def ring_scatter(size, origin, index, up, down, q_out, q_in, r_out, r_in, before):
        part_size = size // 2

        def block(i):
            return origin + i * size

        def post_slots(k, start, to, behind=None):
            def one(s, _):
                x = acc[start + s]
                if behind is not None:
                    x = x + decode(q_in[behind, s], r_in[behind, s])
                q_out[k, s], r_out[k, s] = encode(x)
                return 0

            lax.fori_loop(0, part_size, one, 0)
            copies = send(q_out.at[k], q_in.at[k], to), send(r_out.at[k], r_in.at[k], to)
            for copy in copies:
                copy.start()
            return copies

        far = block(near(index, 2))
        above, below = block(near(index, 1)), block(near(index, -1))
        before(2)
        u1 = post_slots(0, far, up)
        d1 = post_slots(1, far + part_size, down)
        yield
        before(1)
        u2 = post_slots(2, above + part_size, up)
        before(-1)
        d2 = post_slots(3, below, down)
        before(0)
        yield
        arrived(u1)
        u3 = post_slots(4, above, up, 0)
        arrived(d1)
        d3 = post_slots(5, below + part_size, down, 1)
        yield
        arrived(u2 + d2 + u3 + d3)
        keep = block(index)

        def one(s, _):
            for first_k, second_k, at_s in ((4, 3, s), (2, 5, s + part_size)):
                acc[keep + at_s] = (
                    acc[keep + at_s]
                    + decode(q_in[first_k, s], r_in[first_k, s])
                    + decode(q_in[second_k, s], r_in[second_k, s])
                )
            return 0

        lax.fori_loop(0, part_size, one, 0)
        yield

    def add_core(by):
        core_copies[(2, 1, -1, 0).index(by)].wait_recv()
        start = near(b, by) * 16
        add_into(acc, start, core_in, start, 16)

    over_b = ring_scatter(16, 0, b, up_b, down_b, bq_out, bq_in, br_out, br_in, add_core)
    next(over_b)

    def to_near(i, _):
        way, j = div(i, 2), rem(i, 2)
        post(way, 2 + j, partial(1 + 2 * way, (1 - way) * 2 + j))
        return 0

    lax.fori_loop(0, 4, to_near, 0)

    next(over_b)

    def rest(i, _):
        joint[i] = partial(1 + 2 * div(i, 2), i)
        own[i] = partial(0, i)
        return 0

    lax.fori_loop(0, 4, rest, 0)


    def pass_on(i, _):
        way, j = div(i, 2), rem(i, 2)
        for copy in message(way, j):
            copy.wait_recv()
        post(way, 4 + j, joint[i] + received(way, j))
        return 0

    lax.fori_loop(0, 4, pass_on, 0)
    puts = [grad_input(0)]
    next(over_b)
    puts += [grad_input(1)]
    next(over_b)
    for _ in ring_scatter(4, b * 16, a, up_a, down_a, aq_out, aq_in, ar_out, ar_in, lambda by: None):
        pass
    kept = b * 16 + a * 4
    zl_copy = send(acc.at[pl.ds(kept + 2 * (1 - zl), 2)], zl_in, other_zl)
    zl_copy.start()

    def finish(i, _):
        h, j = div(i, 2), rem(i, 2)
        from_left, from_right = 4 - 2 * h + j, 2 + 2 * h + j
        for copy in message(0, from_left) + message(1, from_right):
            copy.wait_recv()
        total = own[i] + received(0, from_left) + received(1, from_right)
        values_ref[rows(i * chunk, chunk, chunk), :] = total.astype(jnp.bfloat16)
        return 0

    lax.fori_loop(0, 4, finish, 0)
    zl_copy.wait_recv()
    for k in range(2):
        tile = acc[kept + 2 * zl + k] + zl_in[k]
        mean = jnp.sum(tile * tile, axis=(0, 1), keepdims=True) / (TILE * TILE)
        update_ref[k] = (tile * lax.rsqrt(mean + 1e-06)).T.astype(jnp.bfloat16)
    for put in puts:
        put.wait()
    for copy in started:
        copy.wait_send()
    for way in range(2):
        for j in range(6):
            for copy in message(way, j):
                copy.wait_send()


COPIES = 61


def hand_over_kernel(parts, *refs):
    count = len(parts)
    sources, targets, held = refs[:count], refs[count : 2 * count], refs[2 * count : 3 * count]
    in_sem, out_sem = refs[3 * count :]
    ins, outs = [], []
    for source, target, hold, number in zip(sources, targets, held, parts):
        size = source.shape[0] // number
        for i in range(number):
            piece, k = pl.ds(i * size, size), len(ins)
            ins.append(pltpu.make_async_copy(source.at[piece], hold.at[piece], in_sem.at[k]))
            outs.append(pltpu.make_async_copy(hold.at[piece], target.at[piece], out_sem.at[k]))
    for copy in ins:
        copy.start()
    for arrival, copy in zip(ins, outs):
        arrival.wait()
        copy.start()
    for copy in outs:
        copy.wait()


def hand_over(results):
    parts = (1, 8, 1)
    shapes = [jax.ShapeDtypeStruct(x.shape, x.dtype) for x in results]
    anywhere = [pl.BlockSpec(memory_space=pl.ANY)] * len(shapes)
    return pl.pallas_call(
        functools.partial(hand_over_kernel, parts),
        out_shape=shapes,
        in_specs=anywhere,
        out_specs=anywhere,
        scratch_shapes=[pltpu.VMEM(x.shape, x.dtype) for x in shapes]
        + [pltpu.SemaphoreType.DMA((sum(parts),))] * 2,
    )(*results)


def local(normed, tile_values, tile_rows, tile_columns, cotangent):
    tokens, features = normed.shape
    width = cotangent.shape[1]
    anywhere = pl.BlockSpec(memory_space=pl.ANY)
    vmem = pl.BlockSpec(memory_space=pltpu.VMEM)
    smem = pl.BlockSpec(memory_space=pltpu.SMEM)
    f32, bf16 = jnp.float32, jnp.bfloat16
    results = pl.pallas_call(
        kernel,
        out_shape=(
            jax.ShapeDtypeStruct((tokens, width), bf16),
            jax.ShapeDtypeStruct((tokens, features), bf16),
            jax.ShapeDtypeStruct((2, TILE, TILE), bf16),
        ),
        in_specs=[anywhere, anywhere, anywhere, smem, smem],
        out_specs=(vmem, anywhere, vmem),
        scratch_shapes=[
            pltpu.VMEM((tokens, features), bf16),
            pltpu.VMEM((RING, tokens, width), bf16),
            pltpu.VMEM((RING, width, tokens), bf16),
            pltpu.VMEM((128, TILE, TILE), bf16),
            pltpu.VMEM((64, 8, TILE), jnp.int32),
            pltpu.VMEM((16, TILE), jnp.int32),
            pltpu.SMEM((16, TILE), jnp.int32),
            pltpu.VMEM((RING, features, width), bf16),
            pltpu.VMEM((4, tokens // 4, width), f32),
            pltpu.VMEM((4, tokens // 4, width), f32),
            pltpu.VMEM((2, 6, tokens // 4, width), jnp.int16),
            pltpu.VMEM((2, 6, tokens // 4, width), jnp.int16),
            pltpu.VMEM((2, 6, 8, width), f32),
            pltpu.VMEM((2, 6, 8, width), f32),
            pltpu.VMEM((128, TILE, TILE), f32),
            pltpu.VMEM((2, 64, TILE, TILE), f32),
            pltpu.VMEM((64, TILE, TILE), f32),
            *[pltpu.VMEM((6, 8, TILE, TILE), jnp.int16)] * 2,
            *[pltpu.VMEM((6, 8, 8, TILE), f32)] * 2,
            *[pltpu.VMEM((6, 2, TILE, TILE), jnp.int16)] * 2,
            *[pltpu.VMEM((6, 2, 8, TILE), f32)] * 2,
            pltpu.VMEM((2, TILE, TILE), f32),
            pltpu.VMEM((tokens, features), bf16),
            pltpu.SemaphoreType.DMA((7,)),
            pltpu.SemaphoreType.DMA((COPIES,)),
            pltpu.SemaphoreType.DMA((COPIES,)),
            *[pltpu.SemaphoreType.DMA((2, 6))] * 4,
        ],
        compiler_params=pltpu.CompilerParams(
            collective_id=0, has_side_effects=True, vmem_limit_bytes=67043328
        ),
    )(normed, cotangent, tile_values.reshape(2, TILE, TILE), tile_rows, tile_columns)
    values, grad_input, update = hand_over(results)
    return values, grad_input, update[None]


def solution(mesh):
    in_specs = (
        P("fsdp", "tensor"),
        P("tensor", "fsdp", None, None),
        P("tensor", "fsdp"),
        P("tensor", "fsdp"),
        P("fsdp", "tensor"),
    )
    out_specs = (P("fsdp", "tensor"), P("fsdp", "tensor"), P("tensor", "fsdp", None, None))
    return jax.shard_map(local, mesh=mesh, in_specs=in_specs, out_specs=out_specs, check_vma=False)
```

```python
import functools

import jax
import jax.numpy as jnp
from jax import lax
from jax.experimental import pallas as pl
from jax.experimental.pallas import tpu as pltpu
from jax.sharding import PartitionSpec as P

MESH = pl.DeviceIdType.MESH
TILE = 128
RING = 4


def rem(value, by):
    return lax.rem(value, jnp.int32(by))


def div(value, by):
    return lax.div(value, jnp.int32(by))


def rows(start, size, unit=16):
    return pl.ds(pl.multiple_of(start, unit), size)


def encode(x):
    groups = x.reshape(8, x.shape[0] // 8, x.shape[1])
    largest = jnp.maximum(jnp.max(jnp.abs(groups), axis=1), 1e-30)
    whole = lax.round(groups * (32767.0 / largest)[:, None, :], lax.RoundingMethod.TO_NEAREST_EVEN)
    return whole.astype(jnp.int32).astype(jnp.int16).reshape(x.shape), largest * (1 / 32767.0)


def decode(coded, scales):
    groups = coded.astype(jnp.int32).astype(jnp.float32).reshape(8, coded.shape[0] // 8, coded.shape[1])
    return (groups * scales[:, None, :]).reshape(coded.shape)


def kernel(
    norm_hbm, cot_hbm, tiles_hbm, rows_ref, columns_ref, values_ref, gi, update_ref,
    norm, cot, cot_t, tiles, places, table, table_s, weight, own, joint, z_out, z_in, s_out, s_in,
    grad, packed, core_in, bq_out, bq_in, br_out, br_in, aq_out, aq_in, ar_out, ar_in, pq_out, pq_in, pr_out, pr_in, local_sem, send_sem, recv_sem,
    z_send, z_recv, s_send, s_recv,
):
    tokens, features = norm.shape
    half = tokens // 2
    f, t = lax.axis_index("fsdp"), lax.axis_index("tensor")
    core, y, x, zl = rem(f, 2), rem(div(f, 2), 4), rem(div(f, 8), 4), div(f, 32)
    a = x + core * (y - x)
    b = y + core * (x - y)
    step_a, step_b = 8 - 6 * core, 2 + 6 * core

    def at(aa, bb, zz):
        return (zz * 32 + aa * step_a + bb * step_b + core, t)

    def near(i, by):
        return rem(i + by + RING, RING)

    right, left = (f, near(t, 1)), (f, near(t, -1))
    up_a, down_a = at(near(a, 1), b, zl), at(near(a, -1), b, zl)
    up_b, down_b = at(a, near(b, 1), zl), at(a, near(b, -1), zl)
    other_zl = at(a, b, 1 - zl)
    other_core = (f + 1 - 2 * core, t)

    count = [0]
    started = []

    def send(src, dst, to):
        i = count[0]
        count[0] += 1
        copy = pltpu.make_async_remote_copy(
            src_ref=src, dst_ref=dst, send_sem=send_sem.at[i], recv_sem=recv_sem.at[i],
            device_id=to, device_id_type=MESH,
        )
        started.append(copy)
        return copy

    get_norm = pltpu.make_async_copy(norm_hbm, norm, local_sem.at[0])
    get_norm.start()
    get_cot = pltpu.make_async_copy(cot_hbm, cot.at[t], local_sem.at[1])
    get_cot.start()
    mine = ((core * RING + b) * RING + a) * 2 + zl
    get_tiles = pltpu.make_async_copy(tiles_hbm, tiles.at[pl.ds(mine * 2, 2)], local_sem.at[2])
    get_tiles.start()
    pairs = [
        jnp.where(columns_ref[0, k] >= 0, rows_ref[0, k] * 8 + columns_ref[0, k], -1) for k in range(2)
    ]
    lane = lax.broadcasted_iota(jnp.int32, (8, TILE), 1)
    slot = lax.broadcasted_iota(jnp.int32, (8, TILE), 0) // 4
    places[mine] = jnp.where(slot == 0, pairs[0], pairs[1])

    barrier = pltpu.get_barrier_semaphore()
    partners = (right, left, up_a, down_a, up_b, down_b, other_zl, other_core)
    for partner in partners:
        pl.semaphore_signal(barrier, inc=1, device_id=partner, device_id_type=MESH)
    pl.semaphore_wait(barrier, len(partners))

    first = (
        send(tiles_hbm, tiles.at[pl.ds(mine * 2, 2)], other_zl),
        send(places.at[mine], places.at[mine], other_zl),
    )
    for copy in first:
        copy.start()
    low, high = pl.ds(0, half), pl.ds(half, half)
    cot_r = [send(cot_hbm.at[h], cot.at[t, h], right) for h in (low, high)]
    cot_l = [send(cot_hbm.at[h], cot.at[t, h], left) for h in (high, low)]
    for copy in first:
        copy.wait_recv()
    for i in range(2):
        cot_r[i].start()
        cot_l[i].start()
    get_tiles.wait()

    def send_owners(start, size, to):
        pieces = tiles.at[pl.ds(start * 2, size * 2)], places.at[pl.ds(start, size)]
        copies = [send(piece, piece, to) for piece in pieces]
        for copy in copies:
            copy.start()
        return copies

    def arrived(copies):
        for copy in copies:
            copy.wait_recv()

    def ring_gather(origin, size, index, up, down):
        def block(i):
            return origin + i * size

        low_at, high_at = block(index), block(index) + size // 2
        ups, downs = [], []
        for to_up, to_down in ((low_at, high_at), (high_at, low_at)):
            ups.append(send_owners(to_up, size // 2, up))
            downs.append(send_owners(to_down, size // 2, down))
        yield
        arrived(ups[0])
        ups += [send_owners(block(near(index, -1)), size // 2, up)]
        arrived(downs[0])
        downs += [send_owners(block(near(index, 1)) + size // 2, size // 2, down)]
        yield
        arrived(ups[1])
        arrived(downs[1])
        yield
        arrived(ups[2])
        arrived(downs[2])
        yield

    def to_core(i):
        return send_owners((core * RING + i) * 8, 8, other_core)

    def turn(q):
        cot_t[q] = cot[q].T

    def gradient(q, start, stop):
        def one(n, _):
            out = jnp.dot(
                cot_t[q], norm[:, rows(n * 256, 256, 256)], preferred_element_type=jnp.float32
            )
            for i in range(2):
                for j in range(2):
                    grad[(n * 2 + i) * 8 + q * 2 + j] = out[
                        j * TILE : (j + 1) * TILE, i * TILE : (i + 1) * TILE
                    ]
            return 0

        lax.fori_loop(start, stop, one, 0)

    steps = features // 256
    left_t, right_t, far_t = near(t, -1), near(t, 1), near(t, 2)
    first_ring = ring_gather((core * RING + b) * 8, 2, a, up_a, down_a)
    next(first_ring)
    get_cot.wait()
    turn(t)
    next(first_ring)
    get_norm.wait()
    gradient(t, 0, steps // 4)
    next(first_ring)
    next(first_ring)
    second_ring = ring_gather(core * RING * 8, 8, b, up_b, down_b)
    next(second_ring)
    across = to_core(b)
    gradient(t, steps // 4, steps)
    cot_r[0].wait_recv()
    pass_r = send(cot.at[left_t, low], cot.at[left_t, low], right)
    pass_r.start()
    cot_l[0].wait_recv()
    pass_l = send(cot.at[right_t, high], cot.at[right_t, high], left)
    pass_l.start()
    next(second_ring)
    next(second_ring)
    across += to_core(near(b, -1)) + to_core(near(b, 1))
    next(second_ring)
    across += to_core(near(b, 2))
    cot_r[1].wait_recv()
    turn(left_t)
    gradient(left_t, 0, steps)
    cot_l[1].wait_recv()
    turn(right_t)
    gradient(right_t, 0, steps)
    arrived(across)


    def place(d, sums):
        pair = places[d]
        where_is = jnp.where(pair == lane, d * 2 + slot + 1, 0)
        pair_of = jnp.where(lane == d * 2 + slot, pair, 0)
        return jnp.maximum(sums[0], where_is), sums[1] + pair_of

    zero = jnp.zeros((8, TILE), jnp.int32)
    where_is, pair_of = lax.fori_loop(0, 64, place, (zero, zero), unroll=8)
    table[0:8, :] = where_is
    table[8:16, :] = pair_of
    get_table = pltpu.make_async_copy(table, table_s, local_sem.at[6])
    get_table.start()
    get_table.wait()

    def assemble(q):
        def one(r, _):
            for j in range(2):
                pair = r * 8 + q * 2 + j
                code = jnp.maximum(table_s[0, pair], table_s[4, pair])
                tile = tiles[jnp.maximum(code, 1) - 1]
                tile = jnp.where(code > 0, tile, jnp.zeros_like(tile))
                weight[q, rows(r * TILE, TILE, TILE), j * TILE : (j + 1) * TILE] = tile
            return 0

        lax.fori_loop(0, features // TILE, one, 0, unroll=2)

    assemble(far_t)

    chunk = tokens // 4

    def partial(rel, c):
        return jnp.dot(
            norm[rows(c * chunk, chunk, chunk), :],
            weight[rem(t + rel, RING)],
            preferred_element_type=jnp.float32,
        )

    def message(way, j):
        to = (f, rem(t + 1 + 2 * way, RING))
        copies = [
            pltpu.make_async_remote_copy(
                src_ref=src.at[way, j], dst_ref=dst.at[way, j], send_sem=send_at.at[way, j],
                recv_sem=recv_at.at[way, j], device_id=to, device_id_type=MESH,
            )
            for src, dst, send_at, recv_at in (
                (z_out, z_in, z_send, z_recv), (s_out, s_in, s_send, s_recv)
            )
        ]
        return copies

    def post(way, j, x):
        z_out[way, j], s_out[way, j] = encode(x)
        for copy in message(way, j):
            copy.start()

    def received(way, j):
        return decode(z_in[way, j], s_in[way, j])

    def to_far(j):
        def one(way, _):
            post(way, j, partial(2, way * 2 + j))
            return 0

        lax.fori_loop(0, 2, one, 0)

    to_far(0)
    to_far(1)

    arrived([pass_r, pass_l])
    turn(far_t)
    gradient(far_t, 0, steps)

    def pack(side, whose, i):
        def one(s, _):
            slot = i * 16 + s
            pair = table_s[8, whose * 64 + slot] + table_s[12, whose * 64 + slot]
            tile = grad[jnp.maximum(pair, 0)]
            packed[side, slot] = jnp.where(pair >= 0, tile, jnp.zeros_like(tile))
            return 0

        lax.fori_loop(0, 16, one, 0, unroll=4)

    core_copies = []
    for by in (2, 1, -1, 0):
        i = near(a, by)
        pack(1, 1 - core, i)
        piece = pl.ds(i * 16, 16)
        copy = send(packed.at[1, piece], core_in.at[piece], other_core)
        copy.start()
        core_copies.append(copy)
    for by in (2, 1, -1, 0):
        pack(0, core, near(b, by))

    def input_block(n, _):
        th, block = div(n, 8), rem(n, 8)
        at_rows = rows(th * half, half, half)
        at_cols = rows(block * 256, 256, 256)
        lhs = jnp.concatenate([cot[q, at_rows, :] for q in range(RING)], axis=1)
        rhs = jnp.concatenate([weight[q, at_cols, :] for q in range(RING)], axis=1)
        out = lax.dot_general(lhs, rhs, (((1,), (1,)), ((), ())), preferred_element_type=jnp.float32)
        gi[at_rows, at_cols] = out.astype(jnp.bfloat16)
        return 0

    def grad_input(th):
        lax.fori_loop(th * 8, th * 8 + 8, input_block, 0)

    def add_into(dst, dst_at, src, src_at, size):
        def one(s, _):
            dst[dst_at + s] = dst[dst_at + s] + src[src_at + s]
            return 0

        lax.fori_loop(0, size, one, 0)

    acc = packed.at[0]

    def ring_scatter(size, origin, index, up, down, q_out, q_in, r_out, r_in, before):
        part_size = size // 2

        def block(i):
            return origin + i * size

        def post_slots(k, start, to, behind=None):
            def one(s, _):
                x = acc[start + s]
                if behind is not None:
                    x = x + decode(q_in[behind, s], r_in[behind, s])
                q_out[k, s], r_out[k, s] = encode(x)
                return 0

            lax.fori_loop(0, part_size, one, 0)
            copies = send(q_out.at[k], q_in.at[k], to), send(r_out.at[k], r_in.at[k], to)
            for copy in copies:
                copy.start()
            return copies

        far = block(near(index, 2))
        above, below = block(near(index, 1)), block(near(index, -1))
        before(2)
        u1 = post_slots(0, far, up)
        d1 = post_slots(1, far + part_size, down)
        yield
        before(1)
        u2 = post_slots(2, above + part_size, up)
        before(-1)
        d2 = post_slots(3, below, down)
        before(0)
        yield
        arrived(u1)
        u3 = post_slots(4, above, up, 0)
        arrived(d1)
        d3 = post_slots(5, below + part_size, down, 1)
        yield
        arrived(u2 + d2 + u3 + d3)
        keep = block(index)

        def one(s, _):
            for first_k, second_k, at_s in ((4, 3, s), (2, 5, s + part_size)):
                acc[keep + at_s] = (
                    acc[keep + at_s]
                    + decode(q_in[first_k, s], r_in[first_k, s])
                    + decode(q_in[second_k, s], r_in[second_k, s])
                )
            return 0

        lax.fori_loop(0, part_size, one, 0)
        yield

    def add_core(by):
        core_copies[(2, 1, -1, 0).index(by)].wait_recv()
        start = near(b, by) * 16
        add_into(acc, start, core_in, start, 16)

    over_b = ring_scatter(16, 0, b, up_b, down_b, bq_out, bq_in, br_out, br_in, add_core)
    next(over_b)

    for q in (left_t, right_t, t):
        assemble(q)

    def to_near(i, _):
        way, j = div(i, 2), rem(i, 2)
        post(way, 2 + j, partial(1 + 2 * way, (1 - way) * 2 + j))
        return 0

    lax.fori_loop(0, 4, to_near, 0)

    next(over_b)

    def rest(i, _):
        joint[i] = partial(1 + 2 * div(i, 2), i)
        own[i] = partial(0, i)
        return 0

    lax.fori_loop(0, 4, rest, 0)


    def pass_on(i, _):
        way, j = div(i, 2), rem(i, 2)
        for copy in message(way, j):
            copy.wait_recv()
        post(way, 4 + j, joint[i] + received(way, j))
        return 0

    lax.fori_loop(0, 4, pass_on, 0)
    grad_input(0)
    next(over_b)
    grad_input(1)
    next(over_b)
    for _ in ring_scatter(4, b * 16, a, up_a, down_a, aq_out, aq_in, ar_out, ar_in, lambda by: None):
        pass
    kept = b * 16 + a * 4

    def for_pair(k, _):
        pq_out[k], pr_out[k] = encode(acc[kept + 2 * (1 - zl) + k])
        return 0

    lax.fori_loop(0, 2, for_pair, 0)
    zl_copies = send(pq_out, pq_in, other_zl), send(pr_out, pr_in, other_zl)
    for copy in zl_copies:
        copy.start()

    def finish(i, _):
        h, j = div(i, 2), rem(i, 2)
        from_left, from_right = 4 - 2 * h + j, 2 + 2 * h + j
        for copy in message(0, from_left) + message(1, from_right):
            copy.wait_recv()
        total = own[i] + received(0, from_left) + received(1, from_right)
        values_ref[rows(i * chunk, chunk, chunk), :] = total.astype(jnp.bfloat16)
        return 0

    lax.fori_loop(0, 4, finish, 0)
    arrived(zl_copies)
    for k in range(2):
        tile = acc[kept + 2 * zl + k] + decode(pq_in[k], pr_in[k])
        mean = jnp.sum(tile * tile, axis=(0, 1), keepdims=True) / (TILE * TILE)
        update_ref[k] = (tile * lax.rsqrt(mean + 1e-06)).T.astype(jnp.bfloat16)
    for copy in started:
        copy.wait_send()
    for way in range(2):
        for j in range(6):
            for copy in message(way, j):
                copy.wait_send()


COPIES = 70


def hand_over_kernel(parts, *refs):
    count = len(parts)
    sources, targets, sem = refs[:count], refs[count : 2 * count], refs[2 * count]
    copies = []
    for source, target, number in zip(sources, targets, parts):
        size = source.shape[0] // number
        for i in range(number):
            piece = pl.ds(i * size, size)
            copies.append(pltpu.make_async_copy(source.at[piece], target.at[piece], sem.at[len(copies)]))
    for copy in copies:
        copy.start()
    for copy in copies:
        copy.wait()


def hand_over(results):
    parts = (1, 4, 1)
    return pl.pallas_call(
        functools.partial(hand_over_kernel, parts),
        out_shape=[jax.ShapeDtypeStruct(x.shape, x.dtype) for x in results],
        in_specs=[pl.BlockSpec(memory_space=pltpu.VMEM)] * len(results),
        out_specs=[pl.BlockSpec(memory_space=pl.ANY)] * len(results),
        scratch_shapes=[pltpu.SemaphoreType.DMA((sum(parts),))],
        compiler_params=pltpu.CompilerParams(vmem_limit_bytes=1 << 20),
    )(*results)


def local(normed, tile_values, tile_rows, tile_columns, cotangent):
    tokens, features = normed.shape
    width = cotangent.shape[1]
    anywhere = pl.BlockSpec(memory_space=pl.ANY)
    vmem = pl.BlockSpec(memory_space=pltpu.VMEM)
    smem = pl.BlockSpec(memory_space=pltpu.SMEM)
    f32, bf16 = jnp.float32, jnp.bfloat16
    results = pl.pallas_call(
        kernel,
        out_shape=(
            pltpu.VMEM((tokens, width), bf16),
            pltpu.VMEM((tokens, features), bf16),
            pltpu.VMEM((2, TILE, TILE), bf16),
        ),
        in_specs=[anywhere, anywhere, anywhere, smem, smem],
        out_specs=(vmem, vmem, vmem),
        scratch_shapes=[
            pltpu.VMEM((tokens, features), bf16),
            pltpu.VMEM((RING, tokens, width), bf16),
            pltpu.VMEM((RING, width, tokens), bf16),
            pltpu.VMEM((128, TILE, TILE), bf16),
            pltpu.VMEM((64, 8, TILE), jnp.int32),
            pltpu.VMEM((16, TILE), jnp.int32),
            pltpu.SMEM((16, TILE), jnp.int32),
            pltpu.VMEM((RING, features, width), bf16),
            pltpu.VMEM((4, tokens // 4, width), f32),
            pltpu.VMEM((4, tokens // 4, width), f32),
            pltpu.VMEM((2, 6, tokens // 4, width), jnp.int16),
            pltpu.VMEM((2, 6, tokens // 4, width), jnp.int16),
            pltpu.VMEM((2, 6, 8, width), f32),
            pltpu.VMEM((2, 6, 8, width), f32),
            pltpu.VMEM((128, TILE, TILE), f32),
            pltpu.VMEM((2, 64, TILE, TILE), f32),
            pltpu.VMEM((64, TILE, TILE), f32),
            *[pltpu.VMEM((6, 8, TILE, TILE), jnp.int16)] * 2,
            *[pltpu.VMEM((6, 8, 8, TILE), f32)] * 2,
            *[pltpu.VMEM((6, 2, TILE, TILE), jnp.int16)] * 2,
            *[pltpu.VMEM((6, 2, 8, TILE), f32)] * 2,
            *[pltpu.VMEM((2, TILE, TILE), jnp.int16)] * 2,
            *[pltpu.VMEM((2, 8, TILE), f32)] * 2,
            pltpu.SemaphoreType.DMA((7,)),
            pltpu.SemaphoreType.DMA((COPIES,)),
            pltpu.SemaphoreType.DMA((COPIES,)),
            *[pltpu.SemaphoreType.DMA((2, 6))] * 4,
        ],
        compiler_params=pltpu.CompilerParams(
            collective_id=0, has_side_effects=True, vmem_limit_bytes=50 << 20
        ),
    )(normed, cotangent, tile_values.reshape(2, TILE, TILE), tile_rows, tile_columns)
    values, grad_input, update = hand_over(results)
    return values, grad_input, update[None]


def solution(mesh):
    in_specs = (
        P("fsdp", "tensor"),
        P("tensor", "fsdp", None, None),
        P("tensor", "fsdp"),
        P("tensor", "fsdp"),
        P("fsdp", "tensor"),
    )
    out_specs = (P("fsdp", "tensor"), P("fsdp", "tensor"), P("tensor", "fsdp", None, None))
    return jax.shard_map(local, mesh=mesh, in_specs=in_specs, out_specs=out_specs, check_vma=False)
```

```python
import functools

import jax
import jax.numpy as jnp
from jax import lax
from jax.experimental import pallas as pl
from jax.experimental.pallas import tpu as pltpu
from jax.sharding import PartitionSpec as P

MESH = pl.DeviceIdType.MESH
TILE = 128
RING = 4


def rem(value, by):
    return lax.rem(value, jnp.int32(by))


def div(value, by):
    return lax.div(value, jnp.int32(by))


def rows(start, size, unit=16):
    return pl.ds(pl.multiple_of(start, unit), size)


def encode(x, count=8):
    groups = x.reshape(count, x.shape[0] // count, x.shape[1])
    largest = jnp.maximum(jnp.max(jnp.abs(groups), axis=1), 1e-30)
    whole = lax.round(groups * (32767.0 / largest)[:, None, :], lax.RoundingMethod.TO_NEAREST_EVEN)
    return whole.astype(jnp.int32).astype(jnp.int16).reshape(x.shape), largest * (1 / 32767.0)


def decode(coded, scales):
    groups = coded.astype(jnp.int32).astype(jnp.float32).reshape(
        scales.shape[0], coded.shape[0] // scales.shape[0], coded.shape[1]
    )
    return (groups * scales[:, None, :]).reshape(coded.shape)


def kernel(
    norm_hbm, cot_hbm, tiles_hbm, rows_ref, columns_ref, values_ref, gi, update_ref,
    norm, cot, cot_t, tiles, places, table, table_s, weight, own, joint, z_out, z_in, s_out, s_in,
    grad, packed, core_in, bq_out, bq_in, br_out, br_in, aq_out, aq_in, ar_out, ar_in, pq_out, pq_in, pr_out, pr_in, local_sem, send_sem, recv_sem,
    z_send, z_recv, s_send, s_recv,
):
    tokens, features = norm.shape
    half = tokens // 2
    f, t = lax.axis_index("fsdp"), lax.axis_index("tensor")
    core, y, x, zl = rem(f, 2), rem(div(f, 2), 4), rem(div(f, 8), 4), div(f, 32)
    a = x + core * (y - x)
    b = y + core * (x - y)
    step_a, step_b = 8 - 6 * core, 2 + 6 * core

    def at(aa, bb, zz):
        return (zz * 32 + aa * step_a + bb * step_b + core, t)

    def near(i, by):
        return rem(i + by + RING, RING)

    right, left = (f, near(t, 1)), (f, near(t, -1))
    up_a, down_a = at(near(a, 1), b, zl), at(near(a, -1), b, zl)
    up_b, down_b = at(a, near(b, 1), zl), at(a, near(b, -1), zl)
    other_zl = at(a, b, 1 - zl)
    other_core = (f + 1 - 2 * core, t)

    count = [0]
    started = []

    def send(src, dst, to):
        i = count[0]
        count[0] += 1
        copy = pltpu.make_async_remote_copy(
            src_ref=src, dst_ref=dst, send_sem=send_sem.at[i], recv_sem=recv_sem.at[i],
            device_id=to, device_id_type=MESH,
        )
        started.append(copy)
        return copy

    get_norm = pltpu.make_async_copy(norm_hbm, norm, local_sem.at[0])
    get_norm.start()
    get_cot = pltpu.make_async_copy(cot_hbm, cot.at[t], local_sem.at[1])
    get_cot.start()
    mine = ((core * RING + b) * RING + a) * 2 + zl
    get_tiles = pltpu.make_async_copy(tiles_hbm, tiles.at[pl.ds(mine * 2, 2)], local_sem.at[2])
    get_tiles.start()
    pairs = [
        jnp.where(columns_ref[0, k] >= 0, rows_ref[0, k] * 8 + columns_ref[0, k], -1) for k in range(2)
    ]
    lane = lax.broadcasted_iota(jnp.int32, (8, TILE), 1)
    slot = lax.broadcasted_iota(jnp.int32, (8, TILE), 0) // 4
    places[mine] = jnp.where(slot == 0, pairs[0], pairs[1])

    barrier = pltpu.get_barrier_semaphore()
    partners = (right, left, up_a, down_a, up_b, down_b, other_zl, other_core)
    for partner in partners:
        pl.semaphore_signal(barrier, inc=1, device_id=partner, device_id_type=MESH)
    pl.semaphore_wait(barrier, len(partners))

    first = (
        send(tiles_hbm, tiles.at[pl.ds(mine * 2, 2)], other_zl),
        send(places.at[mine], places.at[mine], other_zl),
    )
    for copy in first:
        copy.start()
    low, high = pl.ds(0, half), pl.ds(half, half)
    cot_r = [send(cot_hbm.at[h], cot.at[t, h], right) for h in (low, high)]
    cot_l = [send(cot_hbm.at[h], cot.at[t, h], left) for h in (high, low)]
    for copy in first:
        copy.wait_recv()
    for i in range(2):
        cot_r[i].start()
        cot_l[i].start()
    get_tiles.wait()

    def send_owners(start, size, to):
        pieces = tiles.at[pl.ds(start * 2, size * 2)], places.at[pl.ds(start, size)]
        copies = [send(piece, piece, to) for piece in pieces]
        for copy in copies:
            copy.start()
        return copies

    def arrived(copies):
        for copy in copies:
            copy.wait_recv()

    def ring_gather(origin, size, index, up, down):
        def block(i):
            return origin + i * size

        low_at, high_at = block(index), block(index) + size // 2
        ups, downs = [], []
        for to_up, to_down in ((low_at, high_at), (high_at, low_at)):
            ups.append(send_owners(to_up, size // 2, up))
            downs.append(send_owners(to_down, size // 2, down))
        yield
        arrived(ups[0])
        ups += [send_owners(block(near(index, -1)), size // 2, up)]
        arrived(downs[0])
        downs += [send_owners(block(near(index, 1)) + size // 2, size // 2, down)]
        yield
        arrived(ups[1])
        arrived(downs[1])
        yield
        arrived(ups[2])
        arrived(downs[2])
        yield

    def to_core(i):
        return send_owners((core * RING + i) * 8, 8, other_core)

    def turn(q):
        cot_t[q] = cot[q].T

    def gradient(q, start, stop):
        def one(n, _):
            out = jnp.dot(
                cot_t[q], norm[:, rows(n * 256, 256, 256)], preferred_element_type=jnp.float32
            )
            for i in range(2):
                for j in range(2):
                    grad[(n * 2 + i) * 8 + q * 2 + j] = out[
                        j * TILE : (j + 1) * TILE, i * TILE : (i + 1) * TILE
                    ]
            return 0

        lax.fori_loop(start, stop, one, 0)

    steps = features // 256
    left_t, right_t, far_t = near(t, -1), near(t, 1), near(t, 2)
    first_ring = ring_gather((core * RING + b) * 8, 2, a, up_a, down_a)
    next(first_ring)
    get_cot.wait()
    turn(t)
    next(first_ring)
    get_norm.wait()
    gradient(t, 0, steps // 4)
    next(first_ring)
    next(first_ring)
    second_ring = ring_gather(core * RING * 8, 8, b, up_b, down_b)
    next(second_ring)
    across = to_core(b)
    gradient(t, steps // 4, steps)
    cot_r[0].wait_recv()
    pass_r = send(cot.at[left_t, low], cot.at[left_t, low], right)
    pass_r.start()
    cot_l[0].wait_recv()
    pass_l = send(cot.at[right_t, high], cot.at[right_t, high], left)
    pass_l.start()
    next(second_ring)
    next(second_ring)
    across += to_core(near(b, -1)) + to_core(near(b, 1))
    next(second_ring)
    across += to_core(near(b, 2))
    cot_r[1].wait_recv()
    turn(left_t)
    gradient(left_t, 0, steps)
    arrived(across)


    def place(d, sums):
        pair = places[d]
        where_is = jnp.where(pair == lane, d * 2 + slot + 1, 0)
        pair_of = jnp.where(lane == d * 2 + slot, pair, 0)
        return jnp.maximum(sums[0], where_is), sums[1] + pair_of

    zero = jnp.zeros((8, TILE), jnp.int32)
    where_is, pair_of = lax.fori_loop(0, 64, place, (zero, zero), unroll=8)
    table[0:8, :] = where_is
    table[8:16, :] = pair_of
    get_table = pltpu.make_async_copy(table, table_s, local_sem.at[6])
    get_table.start()
    get_table.wait()

    def assemble(q):
        def one(r, _):
            for j in range(2):
                pair = r * 8 + q * 2 + j
                code = jnp.maximum(table_s[0, pair], table_s[4, pair])
                tile = tiles[jnp.maximum(code, 1) - 1]
                tile = jnp.where(code > 0, tile, jnp.zeros_like(tile))
                weight[q, rows(r * TILE, TILE, TILE), j * TILE : (j + 1) * TILE] = tile
            return 0

        lax.fori_loop(0, features // TILE, one, 0, unroll=2)

    assemble(far_t)

    chunk = tokens // 4

    def partial(rel, c):
        return jnp.dot(
            norm[rows(c * chunk, chunk, chunk), :],
            weight[rem(t + rel, RING)],
            preferred_element_type=jnp.float32,
        )

    def message(way, j):
        to = (f, rem(t + 1 + 2 * way, RING))
        copies = [
            pltpu.make_async_remote_copy(
                src_ref=src.at[way, j], dst_ref=dst.at[way, j], send_sem=send_at.at[way, j],
                recv_sem=recv_at.at[way, j], device_id=to, device_id_type=MESH,
            )
            for src, dst, send_at, recv_at in (
                (z_out, z_in, z_send, z_recv), (s_out, s_in, s_send, s_recv)
            )
        ]
        return copies

    def post(way, j, x):
        z_out[way, j], s_out[way, j] = encode(x, 4)
        for copy in message(way, j):
            copy.start()

    def received(way, j):
        return decode(z_in[way, j], s_in[way, j])

    def to_far(j):
        def one(way, _):
            post(way, j, partial(2, way * 2 + j))
            return 0

        lax.fori_loop(0, 2, one, 0)

    to_far(0)
    to_far(1)
    cot_l[1].wait_recv()
    turn(right_t)
    gradient(right_t, 0, steps)

    arrived([pass_r, pass_l])
    turn(far_t)
    gradient(far_t, 0, steps)

    def pack(side, whose, i):
        def one(s, _):
            slot = i * 16 + s
            pair = table_s[8, whose * 64 + slot] + table_s[12, whose * 64 + slot]
            tile = grad[jnp.maximum(pair, 0)]
            packed[side, slot] = jnp.where(pair >= 0, tile, jnp.zeros_like(tile))
            return 0

        lax.fori_loop(0, 16, one, 0, unroll=4)

    core_copies = []
    for by in (2, 1, -1, 0):
        i = near(a, by)
        pack(1, 1 - core, i)
        piece = pl.ds(i * 16, 16)
        copy = send(packed.at[1, piece], core_in.at[piece], other_core)
        copy.start()
        core_copies.append(copy)
    for by in (2, 1, -1, 0):
        pack(0, core, near(b, by))

    def input_block(n, _):
        th, block = div(n, 8), rem(n, 8)
        at_rows = rows(th * half, half, half)
        at_cols = rows(block * 256, 256, 256)
        lhs = jnp.concatenate([cot[q, at_rows, :] for q in range(RING)], axis=1)
        rhs = jnp.concatenate([weight[q, at_cols, :] for q in range(RING)], axis=1)
        out = lax.dot_general(lhs, rhs, (((1,), (1,)), ((), ())), preferred_element_type=jnp.float32)
        gi[at_rows, at_cols] = out.astype(jnp.bfloat16)
        return 0

    def grad_input(start, stop):
        lax.fori_loop(start, stop, input_block, 0)

    def add_into(dst, dst_at, src, src_at, size):
        def one(s, _):
            dst[dst_at + s] = dst[dst_at + s] + src[src_at + s]
            return 0

        lax.fori_loop(0, size, one, 0)

    acc = packed.at[0]

    def ring_scatter(size, origin, index, up, down, q_out, q_in, r_out, r_in, before):
        part_size = size // 2

        def block(i):
            return origin + i * size

        def post_slots(k, start, to, behind=None):
            def one(s, _):
                x = acc[start + s]
                if behind is not None:
                    x = x + decode(q_in[behind, s], r_in[behind, s])
                q_out[k, s], r_out[k, s] = encode(x)
                return 0

            lax.fori_loop(0, part_size, one, 0)
            copies = send(q_out.at[k], q_in.at[k], to), send(r_out.at[k], r_in.at[k], to)
            for copy in copies:
                copy.start()
            return copies

        far = block(near(index, 2))
        above, below = block(near(index, 1)), block(near(index, -1))
        before(2)
        u1 = post_slots(0, far, up)
        d1 = post_slots(1, far + part_size, down)
        yield
        before(1)
        u2 = post_slots(2, above + part_size, up)
        before(-1)
        d2 = post_slots(3, below, down)
        before(0)
        yield
        arrived(u1)
        u3 = post_slots(4, above, up, 0)
        arrived(d1)
        d3 = post_slots(5, below + part_size, down, 1)
        yield
        arrived(u2 + d2 + u3 + d3)
        keep = block(index)

        def one(s, _):
            for first_k, second_k, at_s in ((4, 3, s), (2, 5, s + part_size)):
                acc[keep + at_s] = (
                    acc[keep + at_s]
                    + decode(q_in[first_k, s], r_in[first_k, s])
                    + decode(q_in[second_k, s], r_in[second_k, s])
                )
            return 0

        lax.fori_loop(0, part_size, one, 0)
        yield

    def add_core(by):
        core_copies[(2, 1, -1, 0).index(by)].wait_recv()
        start = near(b, by) * 16
        add_into(acc, start, core_in, start, 16)

    over_b = ring_scatter(16, 0, b, up_b, down_b, bq_out, bq_in, br_out, br_in, add_core)
    for q in (left_t, right_t, t):
        assemble(q)

    def to_near(j):
        def one(way, _):
            post(way, 2 + j, partial(1 + 2 * way, (1 - way) * 2 + j))
            return 0

        lax.fori_loop(0, 2, one, 0)

    to_near(0)
    next(over_b)
    next(over_b)
    to_near(1)
    next(over_b)

    def rest(i, _):
        joint[i] = partial(1 + 2 * div(i, 2), i)
        own[i] = partial(0, i)
        return 0

    lax.fori_loop(0, 4, rest, 0)

    def pass_on(i, _):
        way, j = div(i, 2), rem(i, 2)
        for copy in message(way, j):
            copy.wait_recv()
        post(way, 4 + j, joint[i] + received(way, j))
        return 0

    lax.fori_loop(0, 4, pass_on, 0)
    next(over_b)
    over_a = ring_scatter(4, b * 16, a, up_a, down_a, aq_out, aq_in, ar_out, ar_in, lambda by: None)
    next(over_a)
    next(over_a)
    grad_input(0, 3)
    next(over_a)
    grad_input(3, 6)
    next(over_a)
    kept = b * 16 + a * 4

    def for_pair(k, _):
        pq_out[k], pr_out[k] = encode(acc[kept + 2 * (1 - zl) + k])
        return 0

    lax.fori_loop(0, 2, for_pair, 0)
    zl_copies = send(pq_out, pq_in, other_zl), send(pr_out, pr_in, other_zl)
    for copy in zl_copies:
        copy.start()

    grad_input(6, 16)

    def finish(i, _):
        h, j = div(i, 2), rem(i, 2)
        from_left, from_right = 4 - 2 * h + j, 2 + 2 * h + j
        for copy in message(0, from_left) + message(1, from_right):
            copy.wait_recv()
        total = own[i] + received(0, from_left) + received(1, from_right)
        values_ref[rows(i * chunk, chunk, chunk), :] = total.astype(jnp.bfloat16)
        return 0

    lax.fori_loop(0, 4, finish, 0)
    arrived(zl_copies)
    for k in range(2):
        tile = acc[kept + 2 * zl + k] + decode(pq_in[k], pr_in[k])
        mean = jnp.sum(tile * tile, axis=(0, 1), keepdims=True) / (TILE * TILE)
        update_ref[k] = (tile * lax.rsqrt(mean + 1e-06)).T.astype(jnp.bfloat16)
    for copy in started:
        copy.wait_send()
    for way in range(2):
        for j in range(6):
            for copy in message(way, j):
                copy.wait_send()


COPIES = 70


def hand_over_kernel(parts, *refs):
    count = len(parts)
    sources, targets, sem = refs[:count], refs[count : 2 * count], refs[2 * count]
    copies = []
    for source, target, number in zip(sources, targets, parts):
        size = source.shape[0] // number
        for i in range(number):
            piece = pl.ds(i * size, size)
            copies.append(pltpu.make_async_copy(source.at[piece], target.at[piece], sem.at[len(copies)]))
    for copy in copies:
        copy.start()
    for copy in copies:
        copy.wait()


def hand_over(results):
    parts = (1, 4, 1)
    return pl.pallas_call(
        functools.partial(hand_over_kernel, parts),
        out_shape=[jax.ShapeDtypeStruct(x.shape, x.dtype) for x in results],
        in_specs=[pl.BlockSpec(memory_space=pltpu.VMEM)] * len(results),
        out_specs=[pl.BlockSpec(memory_space=pl.ANY)] * len(results),
        scratch_shapes=[pltpu.SemaphoreType.DMA((sum(parts),))],
        compiler_params=pltpu.CompilerParams(vmem_limit_bytes=1 << 20),
    )(*results)


def local(normed, tile_values, tile_rows, tile_columns, cotangent):
    tokens, features = normed.shape
    width = cotangent.shape[1]
    anywhere = pl.BlockSpec(memory_space=pl.ANY)
    vmem = pl.BlockSpec(memory_space=pltpu.VMEM)
    smem = pl.BlockSpec(memory_space=pltpu.SMEM)
    f32, bf16 = jnp.float32, jnp.bfloat16
    results = pl.pallas_call(
        kernel,
        out_shape=(
            pltpu.VMEM((tokens, width), bf16),
            pltpu.VMEM((tokens, features), bf16),
            pltpu.VMEM((2, TILE, TILE), bf16),
        ),
        in_specs=[anywhere, anywhere, anywhere, smem, smem],
        out_specs=(vmem, vmem, vmem),
        scratch_shapes=[
            pltpu.VMEM((tokens, features), bf16),
            pltpu.VMEM((RING, tokens, width), bf16),
            pltpu.VMEM((RING, width, tokens), bf16),
            pltpu.VMEM((128, TILE, TILE), bf16),
            pltpu.VMEM((64, 8, TILE), jnp.int32),
            pltpu.VMEM((16, TILE), jnp.int32),
            pltpu.SMEM((16, TILE), jnp.int32),
            pltpu.VMEM((RING, features, width), bf16),
            pltpu.VMEM((4, tokens // 4, width), f32),
            pltpu.VMEM((4, tokens // 4, width), f32),
            pltpu.VMEM((2, 6, tokens // 4, width), jnp.int16),
            pltpu.VMEM((2, 6, tokens // 4, width), jnp.int16),
            pltpu.VMEM((2, 6, 4, width), f32),
            pltpu.VMEM((2, 6, 4, width), f32),
            pltpu.VMEM((128, TILE, TILE), f32),
            pltpu.VMEM((2, 64, TILE, TILE), f32),
            pltpu.VMEM((64, TILE, TILE), f32),
            *[pltpu.VMEM((6, 8, TILE, TILE), jnp.int16)] * 2,
            *[pltpu.VMEM((6, 8, 8, TILE), f32)] * 2,
            *[pltpu.VMEM((6, 2, TILE, TILE), jnp.int16)] * 2,
            *[pltpu.VMEM((6, 2, 8, TILE), f32)] * 2,
            *[pltpu.VMEM((2, TILE, TILE), jnp.int16)] * 2,
            *[pltpu.VMEM((2, 8, TILE), f32)] * 2,
            pltpu.SemaphoreType.DMA((7,)),
            pltpu.SemaphoreType.DMA((COPIES,)),
            pltpu.SemaphoreType.DMA((COPIES,)),
            *[pltpu.SemaphoreType.DMA((2, 6))] * 4,
        ],
        compiler_params=pltpu.CompilerParams(
            collective_id=0, has_side_effects=True, vmem_limit_bytes=50 << 20
        ),
    )(normed, cotangent, tile_values.reshape(2, TILE, TILE), tile_rows, tile_columns)
    values, grad_input, update = hand_over(results)
    return values, grad_input, update[None]


def solution(mesh):
    in_specs = (
        P("fsdp", "tensor"),
        P("tensor", "fsdp", None, None),
        P("tensor", "fsdp"),
        P("tensor", "fsdp"),
        P("fsdp", "tensor"),
    )
    out_specs = (P("fsdp", "tensor"), P("fsdp", "tensor"), P("tensor", "fsdp", None, None))
    return jax.shard_map(local, mesh=mesh, in_specs=in_specs, out_specs=out_specs, check_vma=False)
```
